32 devices in a mesh: leaf: 8 (over z, y), sub: 4 (over x, core).
Axes of the slice: x: 2, y: 2, z: 4, core: 2. Of those that a mesh axis runs over, the one named last changes fastest.
Arguments:
- sources: bfloat16 [65536, 64], P(('leaf', 'sub')), may hold values from -6 to 6
- leaf_basis: bfloat16 [256, 256, 64], P(('leaf', 'sub')), may hold values from -0.375 to 0.375
- transfer: float32 [2, 64, 64], replicated, may hold values from -0.625 to 0.625
- coupling: float32 [3, 64, 64], replicated, may hold values from -0.5 to 0.5
- near_blocks: bfloat16 [256, 4, 256, 256], P(('leaf', 'sub')), may hold values from -0.1875 to 0.1875
- near_pattern: int32 [256, 4], P(('leaf', 'sub')), may hold values from 0 to 255, as said below
- far_pattern: int32 [508, 3], replicated, may hold values 0 or 1
Outputs:
- product: bfloat16 [65536, 64], P(('leaf', 'sub'))
The draws below stay inside these ranges and needn't reach their ends.
Inputs may be any that keep to these rules, and one draw needn't show every extreme that they name: near_pattern[i, 0] = i; every entry j has j // 8 - i // 8 equal to 0, 1, -1, 4 or -4.
All inputs are finite; a program needn't handle non-finite values.
Results may differ from the reference program's by a relative error of at most 0.001.
Values may be sent and summed in bfloat16 or wider, within the bound.
A program may use at most 64 MiB of HBM per device.

```python
import jax
import jax.numpy as jnp
from jax import lax

LEAF_PTS = 256
RANK = 64
RHS = 64
NEAR = 4
LEAF_DEV = 8
SUB_SPAN = 4
LEAVES = 256
POINTS = 65536
FAR_ROWS = 508


def draw_near_pattern(key, part):
    leaf_ids = jnp.arange(LEAVES, dtype=jnp.int32)
    device_ids = leaf_ids // LEAF_DEV
    device_total = LEAVES // LEAF_DEV
    key_side, key_leaf = jax.random.split(jax.random.fold_in(key, 17))
    direction = jax.random.randint(key_side, (LEAVES, NEAR), 0, 5)
    steps_table = jnp.array([0, -1, 1, -SUB_SPAN, SUB_SPAN], jnp.int32)
    target = device_ids[:, None] + steps_table[direction]
    target = jnp.where((target < 0) | (target >= device_total), device_ids[:, None], target)
    within = jax.random.randint(key_leaf, (LEAVES, NEAR), 0, LEAF_DEV)
    chosen = (target * LEAF_DEV + within).astype(jnp.int32)
    return chosen.at[:, 0].set(leaf_ids)


def touch_ends(values, stream_key, smallest, top_value):
    shape = values.shape
    place = [jax.random.randint(jax.random.fold_in(stream_key, axis), (), 0, shape[axis]) for axis in range(len(shape))]
    values = values.at[tuple(place)].set(smallest)
    longest = shape.index(max(shape))
    place[longest] = (place[longest] + 1) % shape[longest]
    return values.at[tuple(place)].set(top_value)


def levels(own_key, dims, cuts, smallest, largest):
    factor_of, own = 1.0, jax.random.fold_in(own_key, 6)
    for position, blocks in cuts:
        heights = jnp.exp(jax.random.uniform(jax.random.fold_in(own, position), (blocks,), jnp.float32, smallest / len(cuts), largest / len(cuts)))
        factor_of = factor_of * jnp.repeat(heights, dims[position] // blocks).reshape([-1 if axis == position else 1 for axis in range(len(dims))])
    return factor_of


def centred(stream_key, shape, scale, bound, cuts=(), kind=jnp.bfloat16):
    values = scale * jax.random.normal(stream_key, shape, jnp.float32)
    if cuts:
        values = values * levels(stream_key, shape, cuts, -0.22, 0.18)
    return jnp.clip(values, -bound, bound).astype(kind)


def setup_inputs(seed: int = 0) -> dict:
    keys = jax.random.split(jax.random.key(seed), 8)
    return {
        "sources": centred(keys[0], (POINTS, RHS), 1.0, 6.0, ((0, 32),)),
        "leaf_basis": centred(keys[1], (LEAVES, LEAF_PTS, RANK), LEAF_PTS ** -0.5, 0.375, ((0, 32),)),
        "transfer": centred(keys[2], (2, RANK, RANK), (3 * RANK // 2) ** -0.5, 0.625, (), jnp.float32),
        "coupling": centred(keys[3], (3, RANK, RANK), (2 * RANK) ** -0.5, 0.5, (), jnp.float32),
        "near_blocks": centred(keys[4], (LEAVES, NEAR, LEAF_PTS, LEAF_PTS), (NEAR * LEAF_PTS) ** -0.5, 0.1875, ((0, 32),)),
        "near_pattern": draw_near_pattern(jax.random.fold_in(keys[7], 71), 0),
        "far_pattern": touch_ends((jax.random.randint(keys[6], (FAR_ROWS, 3), 0, 3) < 2).astype(jnp.int32), jax.random.fold_in(keys[6], 1), 0, 1),
    }


PRECISE = lax.Precision.HIGHEST


def lift_up(level_vals, transfer):
    paired = level_vals.reshape(-1, 2, level_vals.shape[1], level_vals.shape[2])
    left_part = jnp.einsum('jk,pjr->pkr', transfer[0], paired[:, 0], precision=PRECISE)
    right_part = jnp.einsum('jk,pjr->pkr', transfer[1], paired[:, 1], precision=PRECISE)
    return left_part + right_part


def expand_down(parent_field, transfer):
    first_child = jnp.einsum('kj,pjr->pkr', transfer[0], parent_field, precision=PRECISE)
    second_child = jnp.einsum('kj,pjr->pkr', transfer[1], parent_field, precision=PRECISE)
    stacked = jnp.stack([first_child, second_child], 1)
    return stacked.reshape(-1, parent_field.shape[1], parent_field.shape[2])


def couple_level(level_vals, mask_rows, coupling):
    grouped = level_vals.reshape(-1, 4, level_vals.shape[1], level_vals.shape[2])
    summed = jnp.zeros(level_vals.shape, jnp.float32)
    for offset in range(1, 4):
        shifted = jnp.roll(grouped, -offset, axis=1).reshape(level_vals.shape)
        product_term = jnp.einsum('ab,nbr->nar', coupling[offset - 1], shifted, precision=PRECISE)
        weights = mask_rows[:, offset - 1:offset].astype(jnp.float32)[:, :, None]
        summed = summed + weights * product_term
    return summed


def reference(sources, leaf_basis, transfer, coupling, near_blocks, near_pattern, far_pattern):
    leaf_count = leaf_basis.shape[0]
    points = sources.reshape(leaf_count, LEAF_PTS, RHS).astype(jnp.float32)
    basis_wide = leaf_basis.astype(jnp.float32)
    moments = [jnp.einsum('lpk,lpr->lkr', basis_wide, points, precision=PRECISE)]
    while moments[-1].shape[0] > 4:
        moments.append(lift_up(moments[-1], transfer))
    locals_list = []
    row_start = 0
    for level_vals in moments:
        cluster_count = level_vals.shape[0]
        mask_rows = far_pattern[row_start:row_start + cluster_count]
        locals_list.append(couple_level(level_vals, mask_rows, coupling))
        row_start = row_start + cluster_count
    field_down = locals_list[-1]
    for level_id in range(len(moments) - 2, -1, -1):
        field_down = locals_list[level_id] + expand_down(field_down, transfer)
    far_part = jnp.einsum('lpk,lkr->lpr', basis_wide, field_down, precision=PRECISE)
    device_total = leaf_count // LEAF_DEV
    blocks_grouped = near_blocks.reshape(device_total, LEAF_DEV, NEAR, LEAF_PTS, LEAF_PTS)
    pattern_grouped = near_pattern.reshape(device_total, LEAF_DEV, NEAR)

    def near_one(inputs):
        blocks_here, pattern_here = inputs
        gathered = points[pattern_here]
        return jnp.einsum('lsab,lsbr->lar', blocks_here.astype(jnp.float32), gathered, precision=PRECISE)

    near_part = lax.map(near_one, (blocks_grouped, pattern_grouped)).reshape(leaf_count, LEAF_PTS, RHS)
    return (far_part + near_part).reshape(leaf_count * LEAF_PTS, RHS).astype(jnp.bfloat16)
```

```python
import functools
from contextlib import nullcontext

import jax
import jax.numpy as jnp
from jax import lax
from jax.experimental import pallas as pl
from jax.experimental.pallas import tpu as pltpu
from jax.sharding import PartitionSpec as P

BF = jnp.bfloat16
F32 = jnp.float32
MESH = pl.DeviceIdType.MESH


def mark(name):
    return nullcontext()


def halves(x):
    hi = x.astype(BF)
    return hi, (x - hi.astype(F32)).astype(BF)


def split(x):
    return jnp.concatenate(halves(x), axis=1)


def nt(a, b):
    return lax.dot_general(a, b, (((1,), (1,)), ((), ())), preferred_element_type=F32)


def nn(a, b):
    return jnp.dot(a, b, preferred_element_type=F32)


def fold(y, width):
    return y[:, :width] + y[:, width:]


def kernel(
    cfg, src, basis, transfer_hbm, coupling_hbm, blocks, near_hbm, far_hbm, out,
    buf, bas, nb, buf_a, pair2, buf4, buf5, buf6, wdown, wpath, transfer, coupling,
    near_pat, far_pat, load_sem, halo_send, near_recv, y_recv, z_recv, a_sem, p_sem,
    b_sem, q_sem, known,
):
    sub, devices, leaf_dev, near = cfg
    rank = basis.shape[1]
    rhs = src.shape[0]
    points = basis.shape[2]
    block = 2 * sub
    block_count = devices // block
    me = lax.axis_index("leaf") * sub + lax.axis_index("sub")
    mine = lax.rem(me, block)
    own_block = me // block
    place_sub = lax.rem(me, sub)
    upper = mine // sub
    has_prev = own_block > 0
    has_next = own_block < block_count - 1
    first_sub, last_sub = place_sub == 0, place_sub == sub - 1
    outer = first_sub | last_sub
    lower = upper == 0
    relayed = leaf_dev // 2
    turned = leaf_dev // 2
    head = leaf_dev // 4

    y_slot = 4 - 4 * upper
    z_slot = 4 * upper
    across = me + sub - 2 * sub * upper
    z_step = block - 2 * block * upper
    z_target = me + z_step
    z_send = (lower & has_next) | (jnp.logical_not(lower) & has_prev)
    z_have = (lower & has_prev) | (jnp.logical_not(lower) & has_next)
    beyond = me - sub + 2 * sub * upper
    first_turn = (lower & first_sub) | (jnp.logical_not(lower) & last_sub)
    other_turn = (lower & last_sub) | (jnp.logical_not(lower) & first_sub)
    second_turn = z_have & other_turn
    skip_turn = z_send & other_turn
    skip_target = z_target + (sub - 1) * (2 * upper - 1)
    skip_source = me - (z_step + (sub - 1) * (2 * upper - 1))

    def target(dev):
        return (dev // sub, lax.rem(dev, sub))

    def remote(source, dest, send, recv, dev):
        return pltpu.make_async_remote_copy(
            src_ref=source, dst_ref=dest, send_sem=send, recv_sem=recv,
            device_id=target(dev), device_id_type=MESH,
        )

    barrier = pltpu.get_barrier_semaphore()
    peers = []
    for k in range(1, block):
        peers.append(own_block * block + lax.rem(mine + k, block))

    def greet(semaphore, condition, peer):
        @pl.when(condition)
        def _():
            pl.semaphore_signal(semaphore, inc=1, device_id=target(peer), device_id_type=MESH)

    expected = len(peers) + sum(
        jnp.where(condition, 1, 0) for condition in (has_prev, has_next, z_have, skip_turn)
    )
    for peer in peers:
        pl.semaphore_signal(barrier, inc=1, device_id=target(peer), device_id_type=MESH)
    greet(barrier, has_prev, me - block)
    greet(barrier, has_next, me + block)
    greet(barrier, z_have, beyond)
    greet(barrier, z_have & first_turn, skip_source)

    small_loads = [
        pltpu.make_async_copy(source, dest, load_sem.at[number])
        for number, (source, dest) in enumerate(
            (
                (transfer_hbm, transfer), (coupling_hbm, coupling),
                (near_hbm, near_pat), (far_hbm, far_pat), (basis, bas),
            )
        )
    ]
    for copy in small_loads[:1] + small_loads[4:]:
        copy.start()
    for leaf in range(leaf_dev):
        pltpu.make_async_copy(
            src.at[:, pl.ds(points * leaf, points)], buf.at[2, leaf], load_sem.at[5]
        ).start()
    for copy in small_loads[1:4]:
        copy.start()

    rounds = block_count - 2

    def make_known(r):
        greet(known.at[r - 1, 0], (own_block > 0) & (own_block + r < block_count), me - block)
        greet(known.at[r - 1, 1], (own_block < block_count - 1) & (own_block >= r), me + block)

    def get_known(r):
        @pl.when(own_block + r + 1 < block_count)
        def _():
            pl.semaphore_wait(known.at[r - 1, 0], 1)

        @pl.when(own_block >= r + 1)
        def _():
            pl.semaphore_wait(known.at[r - 1, 1], 1)

    def doubled(parts):
        rows = []
        for part in parts:
            row = split(part)
            rows += [row, row]
        return jnp.concatenate(rows, axis=0)

    with mark("00tc"):
        small_loads[0].wait()
    sides = [transfer[side] for side in range(2)]
    step_weight = jnp.concatenate([doubled([side]) for side in sides], axis=1)
    w_up = {2: doubled(sides)}
    paths = sides
    while len(paths) < max(leaf_dev, block):
        wide = nn(split(jnp.concatenate(paths, axis=0)), step_weight)
        longer = jnp.concatenate(
            [fold(wide[:, : 2 * rank], rank), fold(wide[:, 2 * rank :], rank)], axis=0
        )
        paths = [longer[p * rank : (p + 1) * rank] for p in range(2 * len(paths))]
        w_up[len(paths)] = doubled(paths)

    def lift(parts, span):
        rows = [
            jnp.concatenate(parts[p * span : (p + 1) * span], axis=1)
            for p in range(len(parts) // span)
        ]
        rows = rows[0] if len(rows) == 1 else jnp.concatenate(rows, axis=0)
        lifted = split(fold(nn(rows, w_up[span]), rank))
        return [lifted[p * rhs : (p + 1) * rhs] for p in range(len(parts) // span)]

    def send_across(leaves):
        for leaf in leaves:
            remote(
                src.at[:, pl.ds(points * leaf, points)], buf.at[z_slot, leaf],
                halo_send.at[0], y_recv.at[leaf], across,
            ).start()

    def send_inner():
        send_across(range(relayed))
        for leaf in range(relayed, leaf_dev):
            @pl.when(z_have)
            def _(leaf=leaf):
                remote(
                    src.at[:, pl.ds(points * leaf, points)], buf.at[y_slot, leaf],
                    halo_send.at[5], z_recv.at[leaf], beyond,
                ).start()

            send_across([leaf])

    with mark("03barrier"):
        pl.semaphore_wait(barrier, expected)
    pl.when(outer)(functools.partial(send_across, range(head)))
    with mark("01load"):
        small_loads[4].wait()
        pltpu.make_async_copy(buf.at[2], buf.at[2], load_sem.at[5]).wait()
    with mark("02mom"):
        moment0 = [split(nt(buf[2, leaf], bas[leaf])) for leaf in range(leaf_dev)]
        buf_a[mine] = lift(moment0, leaf_dev)[0]
    with mark("04asend"):
        for k in range(block - 1, 0, -1):
            remote(
                buf_a.at[mine], buf_a.at[mine], a_sem.at[0], a_sem.at[1],
                own_block * block + lax.rem(mine + k, block),
            ).start()

    if rounds > 0:
        make_known(1)

    pl.when(outer)(functools.partial(send_across, range(head, leaf_dev)))
    for number, step in enumerate((1, -1)):
        @pl.when(place_sub < sub - 1 if step > 0 else place_sub > 0)
        def _(number=number, step=step):
            for leaf in range(leaf_dev):
                remote(
                    src.at[:, pl.ds(points * leaf, points)], buf.at[2 - step, leaf],
                    halo_send.at[1 + number], near_recv.at[number], me + step,
                ).start()

    near_loads = [
        pltpu.make_async_copy(blocks.at[leaf], nb.at[leaf], load_sem.at[6])
        for leaf in range(leaf_dev)
    ]
    for copy in near_loads:
        copy.start()

    two = lift(moment0, leaf_dev // 2)
    pair2[0, 0] = two[0]
    pair2[0, 1] = two[1]
    pair_copy = remote(
        pair2.at[0], pair2.at[1], p_sem.at[0], p_sem.at[1], me + 1 - 2 * lax.rem(me, 2)
    )
    pair_copy.start()

    def turn(slot, leaf):
        @pl.when(place_sub == 0)
        def _():
            remote(
                buf.at[slot, leaf], buf.at[3, leaf],
                halo_send.at[4], near_recv.at[1], me + sub - 1,
            ).start()

        @pl.when(place_sub == sub - 1)
        def _():
            remote(
                buf.at[slot, leaf], buf.at[1, leaf],
                halo_send.at[4], near_recv.at[0], me - sub + 1,
            ).start()

    def y_wait(leaf):
        remote(
            buf.at[y_slot, leaf], buf.at[y_slot, leaf], halo_send.at[0], y_recv.at[leaf], across
        ).wait_recv()

    def relay_first(leaf):
        y_wait(leaf)

        @pl.when(z_send)
        def _():
            remote(
                buf.at[y_slot, leaf], buf.at[z_slot, leaf],
                halo_send.at[3], z_recv.at[leaf], z_target,
            ).start()

        @pl.when(first_turn)
        def _():
            turn(y_slot, leaf)

        if leaf >= turned:
            @pl.when(skip_turn & first_sub)
            def _():
                remote(
                    buf.at[y_slot, leaf], buf.at[3, leaf],
                    halo_send.at[6], near_recv.at[1], skip_target,
                ).start()

            @pl.when(skip_turn & last_sub)
            def _():
                remote(
                    buf.at[y_slot, leaf], buf.at[1, leaf],
                    halo_send.at[6], near_recv.at[0], skip_target,
                ).start()

    def z_wait(leaf):
        remote(
            buf.at[z_slot, leaf], buf.at[z_slot, leaf], halo_send.at[3], z_recv.at[leaf], across
        ).wait_recv()

    def relay_second(leaf):
        @pl.when(second_turn)
        def _():
            z_wait(leaf)
            turn(z_slot, leaf)

    row_starts = [0]
    size = leaf_dev * devices
    while size > 4:
        row_starts.append(row_starts[-1] + size)
        size //= 2

    def weight(offset, row):
        return jnp.full((rhs, 2 * rank), far_pat[offset, row].astype(F32), F32).astype(BF)

    for copy in small_loads[1:4]:
        copy.wait()
    c_hi, c_lo = [], []
    for offset in range(3):
        hi, lo = halves(coupling[offset])
        c_hi += [hi, hi]
        c_lo += [lo, lo]
    w_couple = jnp.concatenate(
        [jnp.concatenate(c_hi, axis=1), jnp.concatenate(c_lo, axis=1)], axis=0
    )

    def couple(groups, rows):
        stacked = [
            jnp.concatenate(
                [weight(offset, row) * members[offset] for offset in range(3)], axis=1
            )
            for members, row in zip(groups, rows)
        ]
        stacked = stacked[0] if len(stacked) == 1 else jnp.concatenate(stacked, axis=0)
        return fold(nt(stacked, w_couple), rank)

    for side in range(2):
        hi, lo = halves(sides[side])
        wdown[side] = jnp.concatenate(
            [jnp.concatenate([hi, hi], axis=1), jnp.concatenate([lo, lo], axis=1)], axis=0
        )
    w_down = jnp.concatenate([wdown[0], wdown[1]], axis=0)
    if rounds > 0:
        with mark("06known"):
            get_known(1)
        if rounds > 1:
            make_known(2)

    def descend(field, step):
        return fold(nt(split(field), wdown[lax.rem(me >> step, 2)]), rank)

    def fan_out(field, rows):
        both = nt(split(field), w_down)
        children = []
        for p in range(field.shape[0] // rows):
            row = both[p * rows : (p + 1) * rows]
            children.append(fold(row[:, : 2 * rank], rank))
            children.append(fold(row[:, 2 * rank :], rank))
        return jnp.concatenate(children, axis=0)

    low_levels = leaf_dev.bit_length() - 1
    top_count = len(row_starts) - low_levels - 2
    eye = (
        lax.broadcasted_iota(jnp.int32, (rank, rank), 0)
        == lax.broadcasted_iota(jnp.int32, (rank, rank), 1)
    ).astype(F32)
    chain = eye
    for step in range(top_count, -1, -1):
        if step <= 1:
            chain = descend(chain, step)
        elif step < top_count + 1:
            chain = jnp.concatenate([descend(chain, step), eye], axis=0)
    for _ in range(low_levels):
        chain = fan_out(chain, top_count * rank)
    for leaf in range(leaf_dev):
        for number in range(top_count):
            begin = (leaf * top_count + number) * rank
            piece = split(chain[begin : begin + rank])
            for half in range(2):
                wpath[
                    (2 * number + half) * rank : (2 * number + half + 1) * rank,
                    2 * rank * leaf : 2 * rank * (leaf + 1),
                ] = piece

    def relays(early, late):
        @pl.when(outer)
        def _():
            for step, leaf in early:
                step(leaf)

        if late:
            @pl.when(jnp.logical_not(outer))
            def _():
                for leaf in late:
                    relay_first(leaf)

    ones = [(relay_first, leaf) for leaf in range(leaf_dev)]
    twos = [(relay_second, leaf) for leaf in range(turned)]

    with mark("07relA"):
        relays(ones[:head], [])

    locals_low = []
    level_vals, level_id = moment0, 0
    while (leaf_dev >> level_id) >= 4:
        if level_id:
            level_vals = lift(level_vals, 2)
        count = leaf_dev >> level_id
        locals_low.append(
            couple(
                [
                    [level_vals[c // 4 * 4 + (c + offset) % 4] for offset in range(1, 4)]
                    for c in range(count)
                ],
                [row_starts[level_id] + me * count + c for c in range(count)],
            )
        )
        level_id += 1

    with mark("08inner"):
        pl.when(jnp.logical_not(outer))(send_inner)
    with mark("09arecv"):
        pltpu.make_async_copy(
            buf_a.at[pl.ds(0, block - 1)], buf_a.at[pl.ds(0, block - 1)], a_sem.at[1]
        ).wait()
    eight = [buf_a[p] for p in range(block)]
    buf6[own_block] = lift(eight, block)[0]
    with mark("10known"):
        for r in range(2, rounds + 1):
            get_known(r)
            if r < rounds:
                make_known(r + 1)
    with mark("10bsend"):
        for k in range(block_count - 1, 0, -1):
            remote(
                buf6.at[own_block], buf6.at[own_block], b_sem.at[0], b_sem.at[1],
                lax.rem(own_block + k, block_count) * block + mine,
            ).start()
    five = lift(eight, block // 2)
    for p in range(2):
        buf5[p] = five[p]
    q_copy = remote(
        buf5.at[pl.ds(0, 2)], buf5.at[pl.ds(2, 2)], q_sem.at[0], q_sem.at[1],
        (own_block + 1 - 2 * lax.rem(own_block, 2)) * block + mine,
    )
    q_copy.start()
    with mark("11relC"):
        relays(ones[head : leaf_dev - 2], [])
    for p, part in enumerate(lift(eight, 2)):
        buf4[p] = part

    with mark("12pair"):
        pair_copy.wait()
    members2 = two + [pair2[1, 0], pair2[1, 1]]
    groups = [[members2[(c + offset) % 4] for offset in range(1, 4)] for c in range(2)]
    rows = [row_starts[level_id] + me * 2 + c for c in range(2)]
    level_id += 1
    groups.append(
        [buf_a[upper * sub + lax.rem(place_sub + offset, 4)] for offset in range(1, 4)]
    )
    rows.append(row_starts[level_id] + me)
    groups.append([buf4[lax.rem(mine // 2 + offset, 4)] for offset in range(1, 4)])
    rows.append(row_starts[level_id + 1] + me // 2)
    with mark("13relD"):
        relays(ones[leaf_dev - 2 :] + twos[: turned // 2], [])
    middle = couple(groups, rows)
    locals_low.append(middle[: 2 * rhs])
    field = middle[2 * rhs : 3 * rhs] + descend(middle[3 * rhs :], 0)
    for step in range(len(locals_low) - 1, -1, -1):
        field = locals_low[step] + fan_out(field, rhs)
    with mark("14relE"):
        relays(twos[turned // 2 :], range(relayed))

    with mark("15nearload"):
        pltpu.make_async_copy(nb, nb, load_sem.at[6]).wait()
    with mark("16first"):
        first = [nt(buf[2, leaf], nb[leaf, 0]) for leaf in range(leaf_dev)]
    with mark("18brecv"):
        pltpu.make_async_copy(
            buf6.at[pl.ds(0, block_count - 1)], buf6.at[pl.ds(0, block_count - 1)], b_sem.at[1]
        ).wait()
    with mark("19qwait"):
        q_copy.wait()
    groups = [[buf5[lax.rem(upper + offset, 4)] for offset in range(1, 4)]]
    rows = [row_starts[level_id + 2] + me // sub]
    first_six = level_id + 3
    start, span, level = 0, block_count, first_six
    while True:
        own = own_block >> (level - first_six)
        groups.append(
            [
                buf6[start + own // 4 * 4 + lax.rem(lax.rem(own, 4) + offset, 4)]
                for offset in range(1, 4)
            ]
        )
        rows.append(row_starts[level] + own)
        if span <= 4:
            break
        for p, part in enumerate(lift([buf6[start + p] for p in range(span)], 2)):
            buf6[start + span + p] = part
        start, span, level = start + span, span // 2, level + 1
    groups, rows = groups[::-1], rows[::-1]
    with mark("20top"):
        top = split(couple(groups, rows))
        top = jnp.concatenate([top[p * rhs : (p + 1) * rhs] for p in range(top_count)], axis=1)
        spread = nn(top, wpath[...])
    partial = []
    for leaf in range(leaf_dev):
        whole = split(
            field[leaf * rhs : (leaf + 1) * rhs]
            + fold(spread[:, 2 * rank * leaf : 2 * rank * (leaf + 1)], rank)
        )
        twice = jnp.concatenate([bas[leaf], bas[leaf]], axis=0)
        partial.append(first[leaf] + nn(whole, twice))

    with mark("21zwait"):
        @pl.when(jnp.logical_not(outer))
        def _():
            for leaf in range(relayed, leaf_dev):
                y_wait(leaf)

        @pl.when(z_have & jnp.logical_not(second_turn))
        def _():
            for leaf in range(turned):
                z_wait(leaf)

        @pl.when(z_have)
        def _():
            for leaf in range(turned, leaf_dev):
                z_wait(leaf)

    with mark("22near"):
        for number, step in enumerate((-1, 1)):
            @pl.when(me > 0 if step < 0 else me < devices - 1)
            def _(number=number, step=step):
                pltpu.make_async_copy(
                    buf.at[2 + step], buf.at[2 + step], near_recv.at[number]
                ).wait()
    with mark("23near"):
        for leaf in range(leaf_dev):
            acc = partial[leaf]
            for s in range(1, near):
                index = near_pat[s, leaf]
                gap = index // leaf_dev - me
                place = jnp.where(
                    gap == -sub, 0, jnp.where(gap == -1, 1, jnp.where(gap == 0, 2, jnp.where(gap == 1, 3, 4)))
                )
                acc = acc + nt(buf[place, lax.rem(index, leaf_dev)], nb[leaf, s])
            out[:, points * leaf : points * (leaf + 1)] = acc.astype(out.dtype)

    inner = jnp.logical_not(outer)
    sent = (
        (0, me >= 0, leaf_dev), (1, place_sub < sub - 1, leaf_dev), (2, place_sub > 0, leaf_dev),
        (3, z_send & outer, leaf_dev), (3, z_send & inner, relayed),
        (4, first_turn, leaf_dev), (4, second_turn, turned),
        (5, z_have & inner, leaf_dev - relayed), (6, skip_turn, leaf_dev - turned),
    )
    for number, condition, count in sent:
        @pl.when(condition)
        def _(number=number, count=count):
            pltpu.make_async_copy(
                buf.at[2, pl.ds(0, count)], buf.at[2, pl.ds(0, count)], halo_send.at[number]
            ).wait()
    pltpu.make_async_copy(
        buf_a.at[pl.ds(0, block - 1)], buf_a.at[pl.ds(0, block - 1)], a_sem.at[0]
    ).wait()
    pltpu.make_async_copy(
        buf6.at[pl.ds(0, block_count - 1)], buf6.at[pl.ds(0, block_count - 1)], b_sem.at[0]
    ).wait()


def shards(sizes, sources, leaf_basis, transfer, coupling, near_blocks, near_pattern, far_pattern):
    sub, devices = sizes
    leaf_dev, points, rank = leaf_basis.shape
    rhs = sources.shape[1]
    near = near_blocks.shape[1]
    block = 2 * sub
    block_count = devices // block
    top_count = block_count.bit_length() - 1
    vmem = pl.BlockSpec(memory_space=pltpu.VMEM)
    hbm = pl.BlockSpec(memory_space=pl.ANY)
    dma = pltpu.SemaphoreType.DMA
    result = pl.pallas_call(
        functools.partial(kernel, (sub, devices, leaf_dev, near)),
        out_shape=pltpu.VMEM((rhs, leaf_dev * points), BF),
        in_specs=[hbm] * 7,
        out_specs=vmem,
        scratch_shapes=[
            pltpu.VMEM((5, leaf_dev, rhs, points), BF),
            pltpu.VMEM((leaf_dev, rank, points), BF),
            pltpu.VMEM((leaf_dev, near, points, points), BF),
            pltpu.VMEM((block, rhs, 2 * rank), BF),
            pltpu.VMEM((2, 2, rhs, 2 * rank), BF),
            pltpu.VMEM((4, rhs, 2 * rank), BF),
            pltpu.VMEM((4, rhs, 2 * rank), BF),
            pltpu.VMEM((2 * block_count, rhs, 2 * rank), BF),
            pltpu.VMEM((2, 2 * rank, 2 * rank), BF),
            pltpu.VMEM((2 * top_count * rank, 2 * rank * leaf_dev), BF),
            pltpu.VMEM(transfer.shape, F32),
            pltpu.VMEM(coupling.shape, F32),
            pltpu.SMEM(near_pattern.shape[::-1], jnp.int32),
            pltpu.SMEM(far_pattern.shape[::-1], jnp.int32),
            dma((7,)),
            dma((7,)),
            dma((2,)),
            dma((leaf_dev,)),
            dma((leaf_dev,)),
            dma((2,)),
            dma((2,)),
            dma((2,)),
            dma((2,)),
            pltpu.SemaphoreType.REGULAR((max(block_count - 2, 1), 2)),
        ],
        compiler_params=pltpu.CompilerParams(collective_id=0, has_side_effects=True),
    )(
        sources.T,
        leaf_basis.transpose(0, 2, 1),
        transfer,
        coupling,
        near_blocks,
        near_pattern.T,
        far_pattern.T,
    )
    return result.T


def solution(mesh):
    placed = (
        P(("leaf", "sub"), None),
        P(("leaf", "sub"), None, None),
        P(),
        P(),
        P(("leaf", "sub"), None, None, None),
        P(("leaf", "sub"), None),
        P(),
    )
    sizes = (mesh.shape["sub"], mesh.shape["leaf"] * mesh.shape["sub"])
    return jax.shard_map(
        functools.partial(shards, sizes),
        mesh=mesh, in_specs=placed, out_specs=P(("leaf", "sub"), None), check_vma=False,
    )
```

```python
import functools
from contextlib import nullcontext

import jax
import jax.numpy as jnp
from jax import lax
from jax.experimental import pallas as pl
from jax.experimental.pallas import tpu as pltpu
from jax.sharding import PartitionSpec as P

BF = jnp.bfloat16
F32 = jnp.float32
MESH = pl.DeviceIdType.MESH
PLACE_ONE = (0, 1, 2, 3, 3, 4, 5, 9)
PLACE_TWO = (6, 6, 7, 8, 9, 9, 10, 10)
PLACE_INNER = (6, 7, 8, 9, 10, 10, 10, 10)


def mark(name):
    return nullcontext()


def halves(x):
    hi = x.astype(BF)
    return hi, (x - hi.astype(F32)).astype(BF)


def split(x):
    return jnp.concatenate(halves(x), axis=1)


def nt(a, b):
    return lax.dot_general(a, b, (((1,), (1,)), ((), ())), preferred_element_type=F32)


def nn(a, b):
    return jnp.dot(a, b, preferred_element_type=F32)


def fold(y, width):
    return y[:, :width] + y[:, width:]


def relay_plan(leaves, turned, relayed):
    outer = [[] for _ in range(12)]
    inner = [[] for _ in range(12)]
    for leaf in range(leaves):
        outer[PLACE_ONE[leaf * 8 // leaves]].append((0, leaf))
    for leaf in range(turned):
        outer[PLACE_TWO[leaf * 8 // leaves]].append((1, leaf))
    for leaf in range(relayed):
        inner[PLACE_INNER[leaf * 8 // leaves]].append(leaf)
    return outer, inner


def kernel(
    cfg, src, basis, transfer_hbm, coupling_hbm, blocks, near_hbm, far_hbm, out,
    buf_lo, buf_hi, bas, nb, buf_a, pair2, buf4, buf5, buf6, wdown, wpath, transfer, coupling,
    near_pat, far_pat, load_sem, halo_send, near_recv, y_recv, z_recv, a_sem, p_sem,
    b_sem, q_sem, known,
):
    sub, devices, leaf_dev, near = cfg
    rank = basis.shape[1]
    rhs = src.shape[0]
    points = basis.shape[2]
    block = 2 * sub
    block_count = devices // block
    me = lax.axis_index("leaf") * sub + lax.axis_index("sub")
    mine = lax.rem(me, block)
    own_block = me // block
    place_sub = lax.rem(me, sub)
    upper = mine // sub
    has_prev = own_block > 0
    has_next = own_block < block_count - 1
    first_sub, last_sub = place_sub == 0, place_sub == sub - 1
    outer = first_sub | last_sub
    lower = upper == 0
    relayed = leaf_dev // 4
    turned = leaf_dev // 2
    head = leaf_dev // 4

    y_slot = 4 - 4 * upper
    z_slot = 4 * upper
    across = me + sub - 2 * sub * upper
    z_step = block - 2 * block * upper
    z_target = me + z_step
    z_send = (lower & has_next) | (jnp.logical_not(lower) & has_prev)
    z_have = (lower & has_prev) | (jnp.logical_not(lower) & has_next)
    beyond = me - sub + 2 * sub * upper
    first_turn = (lower & first_sub) | (jnp.logical_not(lower) & last_sub)
    other_turn = (lower & last_sub) | (jnp.logical_not(lower) & first_sub)
    second_turn = z_have & other_turn
    skip_turn = z_send & other_turn
    skip_target = z_target + (sub - 1) * (2 * upper - 1)
    skip_source = me - (z_step + (sub - 1) * (2 * upper - 1))

    def target(dev):
        return (dev // sub, lax.rem(dev, sub))

    def remote(source, dest, send, recv, dev):
        return pltpu.make_async_remote_copy(
            src_ref=source, dst_ref=dest, send_sem=send, recv_sem=recv,
            device_id=target(dev), device_id_type=MESH,
        )

    barrier = pltpu.get_barrier_semaphore()
    peers = []
    for k in range(1, block):
        peers.append(own_block * block + lax.rem(mine + k, block))

    def greet(semaphore, condition, peer):
        @pl.when(condition)
        def _():
            pl.semaphore_signal(semaphore, inc=1, device_id=target(peer), device_id_type=MESH)

    expected = len(peers) + sum(
        jnp.where(condition, 1, 0) for condition in (has_prev, has_next, z_have, skip_turn)
    )
    for peer in peers:
        pl.semaphore_signal(barrier, inc=1, device_id=target(peer), device_id_type=MESH)
    greet(barrier, has_prev, me - block)
    greet(barrier, has_next, me + block)
    greet(barrier, z_have, beyond)
    greet(barrier, z_have & first_turn, skip_source)

    small_loads = [
        pltpu.make_async_copy(source, dest, load_sem.at[number])
        for number, (source, dest) in enumerate(
            (
                (transfer_hbm, transfer), (coupling_hbm, coupling),
                (near_hbm, near_pat), (far_hbm, far_pat), (basis, bas),
            )
        )
    ]
    for copy in small_loads[:1] + small_loads[4:]:
        copy.start()
    bufs = (buf_lo, buf_hi)
    short = points // 2
    middle_leaf = leaf_dev // 2

    def piece(slot, number):
        return bufs[number // middle_leaf].at[slot, pl.ds(2 * (number % middle_leaf), 2)]

    for half in range(2):
        for leaf in range(leaf_dev):
            pltpu.make_async_copy(
                src.at[:, pl.ds(points * leaf + short * half, short)], bufs[half].at[2, leaf],
                load_sem.at[5 + half],
            ).start()
    for copy in small_loads[1:4]:
        copy.start()

    rounds = block_count - 2

    def make_known(r):
        greet(known.at[r - 1, 0], (own_block > 0) & (own_block + r < block_count), me - block)
        greet(known.at[r - 1, 1], (own_block < block_count - 1) & (own_block >= r), me + block)

    def get_known(r):
        @pl.when(own_block + r + 1 < block_count)
        def _():
            pl.semaphore_wait(known.at[r - 1, 0], 1)

        @pl.when(own_block >= r + 1)
        def _():
            pl.semaphore_wait(known.at[r - 1, 1], 1)

    def doubled(parts):
        rows = []
        for part in parts:
            row = split(part)
            rows += [row, row]
        return jnp.concatenate(rows, axis=0)

    with mark("00tc"):
        small_loads[0].wait()
    sides = [transfer[side] for side in range(2)]
    step_weight = jnp.concatenate([doubled([side]) for side in sides], axis=1)
    w_up = {2: doubled(sides)}
    paths = sides
    while len(paths) < max(leaf_dev, block):
        wide = nn(split(jnp.concatenate(paths, axis=0)), step_weight)
        longer = jnp.concatenate(
            [fold(wide[:, : 2 * rank], rank), fold(wide[:, 2 * rank :], rank)], axis=0
        )
        paths = [longer[p * rank : (p + 1) * rank] for p in range(2 * len(paths))]
        w_up[len(paths)] = doubled(paths)

    def lift(parts, span):
        rows = [
            jnp.concatenate(parts[p * span : (p + 1) * span], axis=1)
            for p in range(len(parts) // span)
        ]
        rows = rows[0] if len(rows) == 1 else jnp.concatenate(rows, axis=0)
        lifted = split(fold(nn(rows, w_up[span]), rank))
        return [lifted[p * rhs : (p + 1) * rhs] for p in range(len(parts) // span)]

    def joined(leaf):
        return jnp.concatenate([buf_lo[2, leaf], buf_hi[2, leaf]], axis=1)

    def send_across(leaves):
        for leaf in leaves:
            remote(
                piece(2, leaf), piece(z_slot, leaf),
                halo_send.at[0], y_recv.at[leaf], across,
            ).start()

    def send_beyond(leaves):
        for leaf in leaves:
            remote(
                piece(2, leaf), piece(y_slot, leaf),
                halo_send.at[5], z_recv.at[leaf], beyond,
            ).start()

    with mark("01src"):
        for half in range(2):
            pltpu.make_async_copy(
                bufs[half].at[2], bufs[half].at[2], load_sem.at[5 + half]
            ).wait()
    with mark("03barrier"):
        pl.semaphore_wait(barrier, expected)
    pl.when(outer)(functools.partial(send_across, range(head)))
    with mark("01load"):
        small_loads[4].wait()
    with mark("02mom"):
        moment0 = [split(nt(joined(leaf), bas[leaf])) for leaf in range(leaf_dev)]
        buf_a[mine] = lift(moment0, leaf_dev)[0]
    with mark("04asend"):
        for k in [block - 2 * k for k in range(1, block // 2)] + [1]:
            remote(
                buf_a.at[mine], buf_a.at[mine], a_sem.at[0], a_sem.at[2 if k == 1 else 1],
                own_block * block + (mine ^ k),
            ).start()

    if rounds > 0:
        make_known(1)

    pl.when(outer)(functools.partial(send_across, range(head, leaf_dev)))
    for number, step in enumerate((1, -1)):
        @pl.when(place_sub < sub - 1 if step > 0 else place_sub > 0)
        def _(number=number, step=step):
            for leaf in range(leaf_dev):
                remote(
                    piece(2, leaf), piece(2 - step, leaf),
                    halo_send.at[1 + number], near_recv.at[number, leaf // middle_leaf], me + step,
                ).start()

    near_loads = [
        pltpu.make_async_copy(blocks.at[leaf], nb.at[leaf], load_sem.at[7])
        for leaf in range(leaf_dev)
    ]
    for copy in near_loads:
        copy.start()

    two = lift(moment0, leaf_dev // 2)
    pair2[0, 0] = two[0]
    pair2[0, 1] = two[1]
    pair_copy = remote(
        pair2.at[0], pair2.at[1], p_sem.at[0], p_sem.at[1], me + 1 - 2 * lax.rem(me, 2)
    )
    pair_copy.start()

    def turn(slot, leaf):
        @pl.when(place_sub == 0)
        def _():
            remote(
                piece(slot, leaf), piece(3, leaf),
                halo_send.at[4], near_recv.at[1, leaf // middle_leaf], me + sub - 1,
            ).start()

        @pl.when(place_sub == sub - 1)
        def _():
            remote(
                piece(slot, leaf), piece(1, leaf),
                halo_send.at[4], near_recv.at[0, leaf // middle_leaf], me - sub + 1,
            ).start()

    def y_wait(leaf):
        remote(
            piece(y_slot, leaf), piece(y_slot, leaf), halo_send.at[0], y_recv.at[leaf], across
        ).wait_recv()

    def relay_first(leaf):
        with mark(f"y{leaf}"):
            y_wait(leaf)

        @pl.when(z_send)
        def _():
            remote(
                piece(y_slot, leaf), piece(z_slot, leaf),
                halo_send.at[3], z_recv.at[leaf], z_target,
            ).start()

        @pl.when(first_turn)
        def _():
            turn(y_slot, leaf)

        if leaf >= turned:
            @pl.when(skip_turn & first_sub)
            def _():
                remote(
                    piece(y_slot, leaf), piece(3, leaf),
                    halo_send.at[6], near_recv.at[1, leaf // middle_leaf], skip_target,
                ).start()

            @pl.when(skip_turn & last_sub)
            def _():
                remote(
                    piece(y_slot, leaf), piece(1, leaf),
                    halo_send.at[6], near_recv.at[0, leaf // middle_leaf], skip_target,
                ).start()

    def z_wait(leaf):
        remote(
            piece(z_slot, leaf), piece(z_slot, leaf), halo_send.at[3], z_recv.at[leaf], across
        ).wait_recv()

    def relay_second(leaf):
        @pl.when(second_turn)
        def _():
            with mark(f"z{leaf}"):
                z_wait(leaf)
            turn(z_slot, leaf)

    row_starts = [0]
    size = leaf_dev * devices
    while size > 4:
        row_starts.append(row_starts[-1] + size)
        size //= 2

    def weight(offset, row):
        return jnp.full((rhs, 2 * rank), far_pat[offset, row].astype(F32), F32).astype(BF)

    for copy in small_loads[1:4]:
        copy.wait()
    c_hi, c_lo = [], []
    for offset in range(3):
        hi, lo = halves(coupling[offset])
        c_hi += [hi, hi]
        c_lo += [lo, lo]
    w_couple = jnp.concatenate(
        [jnp.concatenate(c_hi, axis=1), jnp.concatenate(c_lo, axis=1)], axis=0
    )

    def couple(groups, rows):
        stacked = [
            jnp.concatenate(
                [weight(offset, row) * members[offset] for offset in range(3)], axis=1
            )
            for members, row in zip(groups, rows)
        ]
        stacked = stacked[0] if len(stacked) == 1 else jnp.concatenate(stacked, axis=0)
        return fold(nt(stacked, w_couple), rank)

    for side in range(2):
        hi, lo = halves(sides[side])
        wdown[side] = jnp.concatenate(
            [jnp.concatenate([hi, hi], axis=1), jnp.concatenate([lo, lo], axis=1)], axis=0
        )
    w_down = jnp.concatenate([wdown[0], wdown[1]], axis=0)
    def descend(field, step):
        return fold(nt(split(field), wdown[lax.rem(me >> step, 2)]), rank)

    def fan_out(field, rows):
        both = nt(split(field), w_down)
        children = []
        for p in range(field.shape[0] // rows):
            row = both[p * rows : (p + 1) * rows]
            children.append(fold(row[:, : 2 * rank], rank))
            children.append(fold(row[:, 2 * rank :], rank))
        return jnp.concatenate(children, axis=0)

    low_levels = leaf_dev.bit_length() - 1
    top_count = len(row_starts) - low_levels - 2
    eye = (
        lax.broadcasted_iota(jnp.int32, (rank, rank), 0)
        == lax.broadcasted_iota(jnp.int32, (rank, rank), 1)
    ).astype(F32)
    chain = eye
    for step in range(top_count, -1, -1):
        if step <= 1:
            chain = descend(chain, step)
        elif step < top_count + 1:
            chain = jnp.concatenate([descend(chain, step), eye], axis=0)
    for _ in range(low_levels):
        chain = fan_out(chain, top_count * rank)
    for leaf in range(leaf_dev):
        for number in range(top_count):
            begin = (leaf * top_count + number) * rank
            both = split(chain[begin : begin + rank])
            for half in range(2):
                wpath[
                    (2 * number + half) * rank : (2 * number + half + 1) * rank,
                    2 * rank * leaf : 2 * rank * (leaf + 1),
                ] = both

    ones = [(relay_first, leaf) for leaf in range(leaf_dev)]
    twos = [(relay_second, leaf) for leaf in range(turned)]
    plan_outer, plan_inner = relay_plan(leaf_dev, turned, relayed)

    def relays(point):
        early = [ones[leaf] if kind == 0 else twos[leaf] for kind, leaf in plan_outer[point]]
        if early:
            @pl.when(outer)
            def _():
                for step, leaf in early:
                    step(leaf)

        late = plan_inner[point]
        if late:
            @pl.when(jnp.logical_not(outer))
            def _():
                for leaf in late:
                    relay_first(leaf)

    if rounds > 0:
        with mark("06known"):
            get_known(1)
        if rounds > 1:
            make_known(2)
    with mark("07p0"):
        relays(0)

    locals_low = []
    level_vals, level_id = moment0, 0
    while (leaf_dev >> level_id) >= 4:
        if level_id:
            level_vals = lift(level_vals, 2)
        count = leaf_dev >> level_id
        locals_low.append(
            couple(
                [
                    [level_vals[c // 4 * 4 + (c + offset) % 4] for offset in range(1, 4)]
                    for c in range(count)
                ],
                [row_starts[level_id] + me * count + c for c in range(count)],
            )
        )
        level_id += 1
        if level_id == 1:
            with mark("08inner"):
                pl.when(jnp.logical_not(outer))(functools.partial(send_across, range(leaf_dev)))
            with mark("08p1"):
                relays(1)
            with mark("09arecv"):
                pltpu.make_async_copy(
                    buf_a.at[pl.ds(0, block // 2 - 1)], buf_a.at[pl.ds(0, block // 2 - 1)],
                    a_sem.at[1],
                ).wait()
            for k in range(2, block, 2):
                remote(
                    buf_a.at[mine ^ k], buf_a.at[mine ^ k], a_sem.at[0], a_sem.at[2], me ^ 1
                ).start()

    with mark("08p2"):
        relays(2)
    with mark("09brecv"):
        pltpu.make_async_copy(
            buf_a.at[pl.ds(0, block // 2)], buf_a.at[pl.ds(0, block // 2)], a_sem.at[2]
        ).wait()
    eight = [buf_a[p] for p in range(block)]
    buf6[own_block] = lift(eight, block)[0]
    with mark("10known"):
        for r in range(2, rounds + 1):
            get_known(r)
            if r < rounds:
                make_known(r + 1)
    with mark("10bsend"):
        for k in range(block_count - 1, 1, -1):
            remote(
                buf6.at[own_block], buf6.at[own_block], b_sem.at[0], b_sem.at[1],
                (own_block ^ k) * block + mine,
            ).start()
    with mark("11p3"):
        relays(3)
    five = lift(eight, block // 2)
    for p in range(2):
        buf5[p] = five[p]
    q_copy = remote(
        buf5.at[pl.ds(0, 2)], buf5.at[pl.ds(2, 2)], q_sem.at[0], q_sem.at[1],
        (own_block + 1 - 2 * lax.rem(own_block, 2)) * block + mine,
    )
    q_copy.start()
    pl.when(z_have & jnp.logical_not(outer))(
        functools.partial(send_beyond, range(relayed, leaf_dev))
    )
    with mark("11p4"):
        relays(4)
    for p, part in enumerate(lift(eight, 2)):
        buf4[p] = part

    with mark("12pair"):
        pair_copy.wait()
    members2 = two + [pair2[1, 0], pair2[1, 1]]
    groups = [[members2[(c + offset) % 4] for offset in range(1, 4)] for c in range(2)]
    rows = [row_starts[level_id] + me * 2 + c for c in range(2)]
    level_id += 1
    groups.append(
        [buf_a[upper * sub + lax.rem(place_sub + offset, 4)] for offset in range(1, 4)]
    )
    rows.append(row_starts[level_id] + me)
    groups.append([buf4[lax.rem(mine // 2 + offset, 4)] for offset in range(1, 4)])
    rows.append(row_starts[level_id + 1] + me // 2)
    with mark("13p5"):
        relays(5)
    middle = couple(groups, rows)
    locals_low.append(middle[: 2 * rhs])
    field = middle[2 * rhs : 3 * rhs] + descend(middle[3 * rhs :], 0)
    with mark("13p6"):
        relays(6)
    for step in range(len(locals_low) - 1, -1, -1):
        field = locals_low[step] + fan_out(field, rhs)
        with mark("13p7"):
            relays(7 + len(locals_low) - 1 - step)

    with mark("15nearload"):
        pltpu.make_async_copy(nb, nb, load_sem.at[7]).wait()
    with mark("16first"):
        first = [nt(joined(leaf), nb[leaf, 0]) for leaf in range(leaf_dev)]
    with mark("17p10"):
        relays(10)
    with mark("19qwait"):
        q_copy.wait()
    buf6[own_block ^ 1] = lift([buf5[2], buf5[3]], 2)[0]

    def add_far(base):
        with mark("18brecv"):
            pltpu.make_async_copy(
                buf6.at[pl.ds(0, block_count - 2)], buf6.at[pl.ds(0, block_count - 2)], b_sem.at[1]
            ).wait()
        groups = [[buf5[lax.rem(upper + offset, 4)] for offset in range(1, 4)]]
        rows = [row_starts[level_id + 2] + me // sub]
        first_six = level_id + 3
        start, span, level = 0, block_count, first_six
        while True:
            own = own_block >> (level - first_six)
            groups.append(
                [
                    buf6[start + own // 4 * 4 + lax.rem(lax.rem(own, 4) + offset, 4)]
                    for offset in range(1, 4)
                ]
            )
            rows.append(row_starts[level] + own)
            if span <= 4:
                break
            for p, part in enumerate(lift([buf6[start + p] for p in range(span)], 2)):
                buf6[start + span + p] = part
            start, span, level = start + span, span // 2, level + 1
        groups, rows = groups[::-1], rows[::-1]
        with mark("20top"):
            top = split(couple(groups, rows))
            top = jnp.concatenate([top[p * rhs : (p + 1) * rhs] for p in range(top_count)], axis=1)
            spread = nn(top, wpath[...])
        partial = []
        for leaf in range(leaf_dev):
            whole = split(
                field[leaf * rhs : (leaf + 1) * rhs]
                + fold(spread[:, 2 * rank * leaf : 2 * rank * (leaf + 1)], rank)
            )
            twice = jnp.concatenate([bas[leaf], bas[leaf]], axis=0)
            partial.append(base[leaf] + nn(whole, twice))
        return partial

    def add_near(base):
        total = base
        for half in range(2):
            begin = half * middle_leaf
            group = range(begin, begin + middle_leaf)
            with mark(f"21wait{half}"):
                @pl.when(jnp.logical_not(outer))
                def _(group=group):
                    for leaf in group:
                        if leaf >= relayed:
                            y_wait(leaf)

                @pl.when(z_have & jnp.logical_not(second_turn))
                def _(group=group):
                    for leaf in group:
                        if leaf < turned:
                            z_wait(leaf)

                @pl.when(z_have)
                def _(group=group):
                    for leaf in group:
                        if leaf >= turned:
                            z_wait(leaf)

            with mark(f"22near{half}"):
                for number, step in enumerate((-1, 1)):
                    @pl.when(me > 0 if step < 0 else me < devices - 1)
                    def _(number=number, step=step, half=half):
                        pltpu.make_async_copy(
                            bufs[half].at[2 + step], bufs[half].at[2 + step],
                            near_recv.at[number, half],
                        ).wait()
            with mark(f"23sum{half}"):
                added = []
                for leaf in range(leaf_dev):
                    acc = total[leaf]
                    for s in range(1, near):
                        index = near_pat[s, leaf]
                        gap = index // leaf_dev - me
                        place = jnp.where(
                            gap == -sub, 0,
                            jnp.where(
                                gap == -1, 1,
                                jnp.where(gap == 0, 2, jnp.where(gap == 1, 3, 4)),
                            ),
                        )
                        acc = acc + nt(
                            bufs[half][place, lax.rem(index, leaf_dev)],
                            nb[leaf, s, :, short * half : short * (half + 1)],
                        )
                    added.append(acc)
                total = added
        return total

    def store(total):
        for leaf in range(leaf_dev):
            out[:, points * leaf : points * (leaf + 1)] = total[leaf].astype(out.dtype)

    @pl.when(z_have)
    def _():
        store(add_near(add_far(first)))

    @pl.when(jnp.logical_not(z_have))
    def _():
        store(add_far(add_near(first)))

    inner = jnp.logical_not(outer)
    sent = (
        (0, me >= 0, leaf_dev), (1, place_sub < sub - 1, leaf_dev), (2, place_sub > 0, leaf_dev),
        (3, z_send & outer, leaf_dev), (3, z_send & inner, relayed),
        (4, first_turn, leaf_dev), (4, second_turn, turned),
        (5, z_have & inner, leaf_dev - relayed), (6, skip_turn, leaf_dev - turned),
    )
    for number, condition, count in sent:
        @pl.when(condition)
        def _(number=number, count=count):
            pltpu.make_async_copy(
                src.at[:, pl.ds(0, points * count)], src.at[:, pl.ds(0, points * count)],
                halo_send.at[number],
            ).wait()
    pltpu.make_async_copy(
        buf_a.at[pl.ds(0, block - 1)], buf_a.at[pl.ds(0, block - 1)], a_sem.at[0]
    ).wait()
    pltpu.make_async_copy(
        buf6.at[pl.ds(0, block_count - 2)], buf6.at[pl.ds(0, block_count - 2)], b_sem.at[0]
    ).wait()


def shards(sizes, sources, leaf_basis, transfer, coupling, near_blocks, near_pattern, far_pattern):
    sub, devices = sizes
    leaf_dev, points, rank = leaf_basis.shape
    rhs = sources.shape[1]
    near = near_blocks.shape[1]
    block = 2 * sub
    block_count = devices // block
    top_count = block_count.bit_length() - 1
    vmem = pl.BlockSpec(memory_space=pltpu.VMEM)
    hbm = pl.BlockSpec(memory_space=pl.ANY)
    dma = pltpu.SemaphoreType.DMA
    result = pl.pallas_call(
        functools.partial(kernel, (sub, devices, leaf_dev, near)),
        out_shape=pltpu.VMEM((rhs, leaf_dev * points), BF),
        in_specs=[hbm] * 7,
        out_specs=vmem,
        scratch_shapes=[
            pltpu.VMEM((5, leaf_dev, rhs, points // 2), BF),
            pltpu.VMEM((5, leaf_dev, rhs, points // 2), BF),
            pltpu.VMEM((leaf_dev, rank, points), BF),
            pltpu.VMEM((leaf_dev, near, points, points), BF),
            pltpu.VMEM((block, rhs, 2 * rank), BF),
            pltpu.VMEM((2, 2, rhs, 2 * rank), BF),
            pltpu.VMEM((4, rhs, 2 * rank), BF),
            pltpu.VMEM((4, rhs, 2 * rank), BF),
            pltpu.VMEM((2 * block_count, rhs, 2 * rank), BF),
            pltpu.VMEM((2, 2 * rank, 2 * rank), BF),
            pltpu.VMEM((2 * top_count * rank, 2 * rank * leaf_dev), BF),
            pltpu.VMEM(transfer.shape, F32),
            pltpu.VMEM(coupling.shape, F32),
            pltpu.SMEM(near_pattern.shape[::-1], jnp.int32),
            pltpu.SMEM(far_pattern.shape[::-1], jnp.int32),
            dma((8,)),
            dma((7,)),
            dma((2, 2)),
            dma((leaf_dev,)),
            dma((leaf_dev,)),
            dma((3,)),
            dma((2,)),
            dma((2,)),
            dma((2,)),
            pltpu.SemaphoreType.REGULAR((max(block_count - 2, 1), 2)),
        ],
        compiler_params=pltpu.CompilerParams(collective_id=0, has_side_effects=True),
    )(
        sources.T,
        leaf_basis.transpose(0, 2, 1),
        transfer,
        coupling,
        near_blocks,
        near_pattern.T,
        far_pattern.T,
    )
    return result.T


def solution(mesh):
    placed = (
        P(("leaf", "sub"), None),
        P(("leaf", "sub"), None, None),
        P(),
        P(),
        P(("leaf", "sub"), None, None, None),
        P(("leaf", "sub"), None),
        P(),
    )
    sizes = (mesh.shape["sub"], mesh.shape["leaf"] * mesh.shape["sub"])
    return jax.shard_map(
        functools.partial(shards, sizes),
        mesh=mesh, in_specs=placed, out_specs=P(("leaf", "sub"), None), check_vma=False,
    )
```

```python
import functools
from contextlib import nullcontext

import jax
import jax.numpy as jnp
from jax import lax
from jax.experimental import pallas as pl
from jax.experimental.pallas import tpu as pltpu
from jax.sharding import PartitionSpec as P

BF = jnp.bfloat16
F32 = jnp.float32
MESH = pl.DeviceIdType.MESH
PLACE_ONE = (0, 1, 2, 3, 3, 4, 5, 6)
PLACE_TWO = (6, 7, 8, 9, 10, 10, 10, 10)
PLACE_INNER = (6, 7, 8, 9, 10, 10, 10, 10)


def mark(name):
    return nullcontext()


def halves(x):
    hi = x.astype(BF)
    return hi, (x - hi.astype(F32)).astype(BF)


def split(x):
    return jnp.concatenate(halves(x), axis=1)


def nt(a, b):
    return lax.dot_general(a, b, (((1,), (1,)), ((), ())), preferred_element_type=F32)


def nn(a, b):
    return jnp.dot(a, b, preferred_element_type=F32)


def fold(y, width):
    return y[:, :width] + y[:, width:]


def relay_plan(leaves, turned, relayed):
    outer = [[] for _ in range(12)]
    inner = [[] for _ in range(12)]
    for leaf in range(leaves):
        outer[PLACE_ONE[leaf * 8 // leaves]].append((0, leaf))
    for leaf in range(turned):
        outer[PLACE_TWO[leaf * 8 // leaves]].append((1, leaf))
    for leaf in range(relayed):
        inner[PLACE_INNER[leaf * 8 // leaves]].append(leaf)
    return outer, inner


def kernel(
    cfg, src, basis, transfer_hbm, coupling_hbm, blocks, near_hbm, far_hbm, out,
    buf_lo, buf_hi, bas, nb, moment, buf_a, pair2, buf4, buf5, buf6, wdown, wpath, transfer, coupling,
    near_pat, far_pat, load_sem, sent_sem, near_recv, y_recv, z_recv, a_recv, far_recv, known,
):
    sub, devices, leaf_dev, near = cfg
    rank = basis.shape[1]
    rhs = src.shape[0]
    points = basis.shape[2]
    block = 2 * sub
    block_count = devices // block
    me = lax.axis_index("leaf") * sub + lax.axis_index("sub")
    mine = lax.rem(me, block)
    own_block = me // block
    place_sub = lax.rem(me, sub)
    upper = mine // sub
    has_prev = own_block > 0
    has_next = own_block < block_count - 1
    first_sub, last_sub = place_sub == 0, place_sub == sub - 1
    outer = first_sub | last_sub
    lower = upper == 0
    early = lower & (place_sub < sub // 2)
    relayed = leaf_dev // 8
    kept = leaf_dev
    turned = leaf_dev // 2
    head = leaf_dev // 4

    y_slot = 4 - 4 * upper
    z_slot = 4 * upper
    across = me + sub - 2 * sub * upper
    z_step = block - 2 * block * upper
    z_target = me + z_step
    z_send = (lower & has_next) | (jnp.logical_not(lower) & has_prev)
    z_have = (lower & has_prev) | (jnp.logical_not(lower) & has_next)
    beyond = me - sub + 2 * sub * upper
    first_turn = (lower & first_sub) | (jnp.logical_not(lower) & last_sub)
    other_turn = (lower & last_sub) | (jnp.logical_not(lower) & first_sub)
    second_turn = z_have & other_turn
    skip_turn = z_send & other_turn
    skip_target = z_target + (sub - 1) * (2 * upper - 1)
    skip_source = me - (z_step + (sub - 1) * (2 * upper - 1))

    def target(dev):
        return (dev // sub, lax.rem(dev, sub))

    def remote(source, dest, send, recv, dev):
        return pltpu.make_async_remote_copy(
            src_ref=source, dst_ref=dest, send_sem=send, recv_sem=recv,
            device_id=target(dev), device_id_type=MESH,
        )

    barrier = pltpu.get_barrier_semaphore()
    peers = []
    for k in range(1, block):
        peers.append(own_block * block + lax.rem(mine + k, block))

    def greet(semaphore, condition, peer):
        @pl.when(condition)
        def _():
            pl.semaphore_signal(semaphore, inc=1, device_id=target(peer), device_id_type=MESH)

    expected = len(peers) + sum(
        jnp.where(condition, 1, 0) for condition in (has_prev, has_next, z_have, skip_turn)
    )
    for peer in peers:
        pl.semaphore_signal(barrier, inc=1, device_id=target(peer), device_id_type=MESH)
    greet(barrier, has_prev, me - block)
    greet(barrier, has_next, me + block)
    greet(barrier, z_have, beyond)
    greet(barrier, z_have & first_turn, skip_source)

    first_load = pltpu.make_async_copy(transfer_hbm, transfer, load_sem.at[0])
    base_load = pltpu.make_async_copy(basis, bas, load_sem.at[1])
    first_load.start()
    base_load.start()
    small_loads = [
        pltpu.make_async_copy(coupling_hbm, coupling, load_sem.at[1]),
        pltpu.make_async_copy(near_hbm, near_pat, load_sem.at[2]),
        pltpu.make_async_copy(far_hbm, far_pat, load_sem.at[3]),
    ]
    bufs = (buf_lo, buf_hi)
    short = points // 2
    middle_leaf = leaf_dev // 2

    def piece(slot, number):
        return bufs[number // middle_leaf].at[slot, pl.ds(2 * (number % middle_leaf), 2)]

    for half in range(2):
        for leaf in range(leaf_dev):
            pltpu.make_async_copy(
                src.at[:, pl.ds(points * leaf + short * half, short)], bufs[half].at[2, leaf],
                load_sem.at[2 + half],
            ).start()

    rounds = block_count - 2

    def make_known(r):
        greet(known.at[r - 1, 0], (own_block > 0) & (own_block + r < block_count), me - block)
        greet(known.at[r - 1, 1], (own_block < block_count - 1) & (own_block >= r), me + block)

    def get_known(r):
        @pl.when(own_block + r + 1 < block_count)
        def _():
            pl.semaphore_wait(known.at[r - 1, 0], 1)

        @pl.when(own_block >= r + 1)
        def _():
            pl.semaphore_wait(known.at[r - 1, 1], 1)

    def doubled(parts):
        rows = []
        for part in parts:
            row = split(part)
            rows += [row, row]
        return jnp.concatenate(rows, axis=0)

    with mark("00tc"):
        first_load.wait()
    sides = [transfer[side] for side in range(2)]
    step_weight = jnp.concatenate([doubled([side]) for side in sides], axis=1)
    w_up = {2: doubled(sides)}
    paths = sides
    while len(paths) < max(leaf_dev, block):
        wide = nn(split(jnp.concatenate(paths, axis=0)), step_weight)
        longer = jnp.concatenate(
            [fold(wide[:, : 2 * rank], rank), fold(wide[:, 2 * rank :], rank)], axis=0
        )
        paths = [longer[p * rank : (p + 1) * rank] for p in range(2 * len(paths))]
        w_up[len(paths)] = doubled(paths)

    def lift(parts, span):
        rows = [
            jnp.concatenate(parts[p * span : (p + 1) * span], axis=1)
            for p in range(len(parts) // span)
        ]
        rows = rows[0] if len(rows) == 1 else jnp.concatenate(rows, axis=0)
        lifted = split(fold(nn(rows, w_up[span]), rank))
        return [lifted[p * rhs : (p + 1) * rhs] for p in range(len(parts) // span)]

    def joined(leaf):
        return jnp.concatenate([buf_lo[2, leaf], buf_hi[2, leaf]], axis=1)

    def send_across(leaves):
        for leaf in leaves:
            remote(
                piece(2, leaf), piece(z_slot, leaf),
                sent_sem.at[0], y_recv.at[leaf], across,
            ).start()

    def send_beyond(leaves):
        for leaf in leaves:
            remote(
                piece(2, leaf), piece(y_slot, leaf),
                sent_sem.at[0], z_recv.at[min(leaf, turned)], beyond,
            ).start()

    with mark("01src"):
        for half in range(2):
            pltpu.make_async_copy(
                bufs[half].at[2], bufs[half].at[2], load_sem.at[2 + half]
            ).wait()
        base_load.wait()
    for copy in small_loads:
        copy.start()

    def find_moments():
        parts = [split(nt(joined(leaf), bas[leaf])) for leaf in range(leaf_dev)]
        for leaf in range(leaf_dev):
            moment[leaf] = parts[leaf]
        buf_a[mine] = lift(parts, leaf_dev)[0]

    with mark("02early"):
        pl.when(early)(find_moments)
    with mark("03barrier"):
        pl.semaphore_wait(barrier, expected)
    pl.when(outer)(functools.partial(send_across, range(head)))
    with mark("02mom"):
        pl.when(jnp.logical_not(early))(find_moments)
    with mark("04asend"):
        for k in [block - 2 * k for k in range(1, block // 2)] + [1]:
            remote(
                buf_a.at[mine], buf_a.at[mine], sent_sem.at[0], a_recv.at[1 if k == 1 else 0],
                own_block * block + (mine ^ k),
            ).start()

    if rounds > 0:
        make_known(1)

    pl.when(outer)(functools.partial(send_across, range(head, leaf_dev)))
    for number, step in enumerate((1, -1)):
        @pl.when(place_sub < sub - 1 if step > 0 else place_sub > 0)
        def _(number=number, step=step):
            for leaf in range(leaf_dev):
                remote(
                    piece(2, leaf), piece(2 - step, leaf),
                    sent_sem.at[0], near_recv.at[number, leaf // middle_leaf], me + step,
                ).start()

    near_loads = [
        pltpu.make_async_copy(blocks.at[leaf], nb.at[leaf], load_sem.at[0])
        for leaf in range(leaf_dev)
    ]
    for copy in near_loads:
        copy.start()

    moment0 = [moment[leaf] for leaf in range(leaf_dev)]
    two = lift(moment0, leaf_dev // 2)
    pair2[0, 0] = two[0]
    pair2[0, 1] = two[1]
    pair_copy = remote(
        pair2.at[0], pair2.at[1], sent_sem.at[0], far_recv.at[0], me + 1 - 2 * lax.rem(me, 2)
    )
    pair_copy.start()

    def turn(slot, leaf):
        @pl.when(place_sub == 0)
        def _():
            remote(
                piece(slot, leaf), piece(3, leaf),
                sent_sem.at[0], near_recv.at[1, leaf // middle_leaf], me + sub - 1,
            ).start()

        @pl.when(place_sub == sub - 1)
        def _():
            remote(
                piece(slot, leaf), piece(1, leaf),
                sent_sem.at[0], near_recv.at[0, leaf // middle_leaf], me - sub + 1,
            ).start()

    def y_wait(leaf):
        remote(
            piece(y_slot, leaf), piece(y_slot, leaf), sent_sem.at[0], y_recv.at[leaf], across
        ).wait_recv()

    def relay_first(leaf):
        with mark(f"y{leaf}"):
            y_wait(leaf)

        if leaf < kept:
            @pl.when(z_send)
            def _():
                remote(
                    piece(y_slot, leaf), piece(z_slot, leaf),
                    sent_sem.at[0], z_recv.at[min(leaf, turned)], z_target,
                ).start()

        @pl.when(first_turn)
        def _():
            turn(y_slot, leaf)

        if leaf >= turned:
            @pl.when(skip_turn & first_sub)
            def _():
                remote(
                    piece(y_slot, leaf), piece(3, leaf),
                    sent_sem.at[0], near_recv.at[1, leaf // middle_leaf], skip_target,
                ).start()

            @pl.when(skip_turn & last_sub)
            def _():
                remote(
                    piece(y_slot, leaf), piece(1, leaf),
                    sent_sem.at[0], near_recv.at[0, leaf // middle_leaf], skip_target,
                ).start()

    def z_wait(leaf):
        remote(
            piece(z_slot, leaf), piece(z_slot, leaf), sent_sem.at[0], z_recv.at[leaf], across
        ).wait_recv()

    def relay_second(leaf):
        @pl.when(second_turn)
        def _():
            with mark(f"z{leaf}"):
                z_wait(leaf)
            turn(z_slot, leaf)

    row_starts = [0]
    size = leaf_dev * devices
    while size > 4:
        row_starts.append(row_starts[-1] + size)
        size //= 2

    def weight(offset, row):
        return jnp.full((rhs, 2 * rank), far_pat[offset, row].astype(F32), F32).astype(BF)

    for copy in small_loads:
        copy.wait()
    c_hi, c_lo = [], []
    for offset in range(3):
        hi, lo = halves(coupling[offset])
        c_hi += [hi, hi]
        c_lo += [lo, lo]
    w_couple = jnp.concatenate(
        [jnp.concatenate(c_hi, axis=1), jnp.concatenate(c_lo, axis=1)], axis=0
    )

    def couple(groups, rows):
        stacked = [
            jnp.concatenate(
                [weight(offset, row) * members[offset] for offset in range(3)], axis=1
            )
            for members, row in zip(groups, rows)
        ]
        stacked = stacked[0] if len(stacked) == 1 else jnp.concatenate(stacked, axis=0)
        return fold(nt(stacked, w_couple), rank)

    for side in range(2):
        hi, lo = halves(sides[side])
        wdown[side] = jnp.concatenate(
            [jnp.concatenate([hi, hi], axis=1), jnp.concatenate([lo, lo], axis=1)], axis=0
        )
    w_down = jnp.concatenate([wdown[0], wdown[1]], axis=0)
    def descend(field, step):
        return fold(nt(split(field), wdown[lax.rem(me >> step, 2)]), rank)

    def fan_out(field, rows):
        both = nt(split(field), w_down)
        children = []
        for p in range(field.shape[0] // rows):
            row = both[p * rows : (p + 1) * rows]
            children.append(fold(row[:, : 2 * rank], rank))
            children.append(fold(row[:, 2 * rank :], rank))
        return jnp.concatenate(children, axis=0)

    low_levels = leaf_dev.bit_length() - 1
    top_count = len(row_starts) - low_levels - 2
    eye = (
        lax.broadcasted_iota(jnp.int32, (rank, rank), 0)
        == lax.broadcasted_iota(jnp.int32, (rank, rank), 1)
    ).astype(F32)
    chain = eye
    for step in range(top_count, -1, -1):
        if step <= 1:
            chain = descend(chain, step)
        elif step < top_count + 1:
            chain = jnp.concatenate([descend(chain, step), eye], axis=0)
    for _ in range(low_levels):
        chain = fan_out(chain, top_count * rank)
    for leaf in range(leaf_dev):
        for number in range(top_count):
            begin = (leaf * top_count + number) * rank
            both = split(chain[begin : begin + rank])
            for half in range(2):
                wpath[
                    (2 * number + half) * rank : (2 * number + half + 1) * rank,
                    2 * rank * leaf : 2 * rank * (leaf + 1),
                ] = both

    ones = [(relay_first, leaf) for leaf in range(leaf_dev)]
    twos = [(relay_second, leaf) for leaf in range(turned)]
    plan_outer, plan_inner = relay_plan(leaf_dev, turned, relayed)

    def relays(point):
        early = [ones[leaf] if kind == 0 else twos[leaf] for kind, leaf in plan_outer[point]]
        if early:
            @pl.when(outer)
            def _():
                for step, leaf in early:
                    step(leaf)

        late = plan_inner[point]
        if late:
            @pl.when(jnp.logical_not(outer))
            def _():
                for leaf in late:
                    relay_first(leaf)

    if rounds > 0:
        with mark("06known"):
            get_known(1)
        if rounds > 1:
            make_known(2)
    with mark("07p0"):
        relays(0)

    locals_low = []
    level_vals, level_id = moment0, 0
    while (leaf_dev >> level_id) >= 4:
        if level_id:
            level_vals = lift(level_vals, 2)
        count = leaf_dev >> level_id
        locals_low.append(
            couple(
                [
                    [level_vals[c // 4 * 4 + (c + offset) % 4] for offset in range(1, 4)]
                    for c in range(count)
                ],
                [row_starts[level_id] + me * count + c for c in range(count)],
            )
        )
        level_id += 1
        if level_id == 1:
            with mark("08inner"):
                pl.when(jnp.logical_not(outer))(functools.partial(send_across, range(leaf_dev)))
            with mark("08p1"):
                relays(1)
            with mark("09arecv"):
                pltpu.make_async_copy(
                    buf_a.at[pl.ds(0, block // 2 - 1)], buf_a.at[pl.ds(0, block // 2 - 1)],
                    a_recv.at[0],
                ).wait()
            for k in range(2, block, 2):
                remote(
                    buf_a.at[mine ^ k], buf_a.at[mine ^ k], sent_sem.at[0], a_recv.at[1], me ^ 1
                ).start()

    with mark("08p2"):
        relays(2)
    with mark("09brecv"):
        pltpu.make_async_copy(
            buf_a.at[pl.ds(0, block // 2)], buf_a.at[pl.ds(0, block // 2)], a_recv.at[1]
        ).wait()
    eight = [buf_a[p] for p in range(block)]
    buf6[own_block] = lift(eight, block)[0]
    with mark("10known"):
        for r in range(2, rounds + 1):
            get_known(r)
            if r < rounds:
                make_known(r + 1)
    with mark("10bsend"):
        for k in range(block_count - 1, 1, -1):
            remote(
                buf6.at[own_block], buf6.at[own_block], sent_sem.at[0], far_recv.at[1],
                (own_block ^ k) * block + mine,
            ).start()
    with mark("11p3"):
        relays(3)
    five = lift(eight, block // 2)
    for p in range(2):
        buf5[p] = five[p]
    q_copy = remote(
        buf5.at[pl.ds(0, 2)], buf5.at[pl.ds(2, 2)], sent_sem.at[0], far_recv.at[2],
        (own_block + 1 - 2 * lax.rem(own_block, 2)) * block + mine,
    )
    q_copy.start()
    pl.when(z_have & jnp.logical_not(outer))(
        functools.partial(send_beyond, range(relayed, leaf_dev))
    )
    if kept < leaf_dev:
        pl.when(z_have & outer)(functools.partial(send_beyond, range(kept, leaf_dev)))
    with mark("11p4"):
        relays(4)
    for p, part in enumerate(lift(eight, 2)):
        buf4[p] = part

    with mark("12pair"):
        pair_copy.wait_recv()
    members2 = two + [pair2[1, 0], pair2[1, 1]]
    groups = [[members2[(c + offset) % 4] for offset in range(1, 4)] for c in range(2)]
    rows = [row_starts[level_id] + me * 2 + c for c in range(2)]
    level_id += 1
    groups.append(
        [buf_a[upper * sub + lax.rem(place_sub + offset, 4)] for offset in range(1, 4)]
    )
    rows.append(row_starts[level_id] + me)
    groups.append([buf4[lax.rem(mine // 2 + offset, 4)] for offset in range(1, 4)])
    rows.append(row_starts[level_id + 1] + me // 2)
    with mark("13p5"):
        relays(5)
    middle = couple(groups, rows)
    locals_low.append(middle[: 2 * rhs])
    field = middle[2 * rhs : 3 * rhs] + descend(middle[3 * rhs :], 0)
    with mark("13p6"):
        relays(6)
    for step in range(len(locals_low) - 1, -1, -1):
        field = locals_low[step] + fan_out(field, rhs)
        with mark("13p7"):
            relays(7 + len(locals_low) - 1 - step)

    with mark("15nearload"):
        pltpu.make_async_copy(nb, nb, load_sem.at[0]).wait()
    with mark("16first"):
        first = [nt(joined(leaf), nb[leaf, 0]) for leaf in range(leaf_dev)]
    with mark("17p10"):
        relays(10)
    with mark("19qwait"):
        q_copy.wait_recv()
    buf6[own_block ^ 1] = lift([buf5[2], buf5[3]], 2)[0]

    def add_far(base):
        with mark("18brecv"):
            pltpu.make_async_copy(
                buf6.at[pl.ds(0, block_count - 2)], buf6.at[pl.ds(0, block_count - 2)], far_recv.at[1]
            ).wait()
        groups = [[buf5[lax.rem(upper + offset, 4)] for offset in range(1, 4)]]
        rows = [row_starts[level_id + 2] + me // sub]
        first_six = level_id + 3
        start, span, level = 0, block_count, first_six
        while True:
            own = own_block >> (level - first_six)
            groups.append(
                [
                    buf6[start + own // 4 * 4 + lax.rem(lax.rem(own, 4) + offset, 4)]
                    for offset in range(1, 4)
                ]
            )
            rows.append(row_starts[level] + own)
            if span <= 4:
                break
            for p, part in enumerate(lift([buf6[start + p] for p in range(span)], 2)):
                buf6[start + span + p] = part
            start, span, level = start + span, span // 2, level + 1
        groups, rows = groups[::-1], rows[::-1]
        with mark("20top"):
            top = split(couple(groups, rows))
            top = jnp.concatenate([top[p * rhs : (p + 1) * rhs] for p in range(top_count)], axis=1)
            spread = nn(top, wpath[...])
        partial = []
        for leaf in range(leaf_dev):
            whole = split(
                field[leaf * rhs : (leaf + 1) * rhs]
                + fold(spread[:, 2 * rank * leaf : 2 * rank * (leaf + 1)], rank)
            )
            twice = jnp.concatenate([bas[leaf], bas[leaf]], axis=0)
            partial.append(base[leaf] + nn(whole, twice))
        return partial

    def add_near(base):
        total = base
        for half in range(2):
            begin = half * middle_leaf
            group = range(begin, begin + middle_leaf)
            with mark(f"21wait{half}"):
                @pl.when(jnp.logical_not(outer))
                def _(group=group):
                    for leaf in group:
                        if leaf >= relayed:
                            y_wait(leaf)

                @pl.when(z_have & jnp.logical_not(second_turn))
                def _(group=group):
                    for leaf in group:
                        if leaf < turned:
                            z_wait(leaf)

                if half:
                    @pl.when(z_have)
                    def _():
                        count = leaf_dev - turned
                        pltpu.make_async_copy(
                            src.at[:, pl.ds(0, points * count)], src.at[:, pl.ds(0, points * count)],
                            z_recv.at[turned],
                        ).wait()

            with mark(f"22near{half}"):
                for number, step in enumerate((-1, 1)):
                    @pl.when(me > 0 if step < 0 else me < devices - 1)
                    def _(number=number, step=step, half=half):
                        pltpu.make_async_copy(
                            bufs[half].at[2 + step], bufs[half].at[2 + step],
                            near_recv.at[number, half],
                        ).wait()
            with mark(f"23sum{half}"):
                added = []
                for leaf in range(leaf_dev):
                    acc = total[leaf]
                    for s in range(1, near):
                        index = near_pat[s, leaf]
                        gap = index // leaf_dev - me
                        place = jnp.where(
                            gap == -sub, 0,
                            jnp.where(
                                gap == -1, 1,
                                jnp.where(gap == 0, 2, jnp.where(gap == 1, 3, 4)),
                            ),
                        )
                        acc = acc + nt(
                            bufs[half][place, lax.rem(index, leaf_dev)],
                            nb[leaf, s, :, short * half : short * (half + 1)],
                        )
                    added.append(acc)
                total = added
        return total

    def store(total):
        for leaf in range(leaf_dev):
            out[:, points * leaf : points * (leaf + 1)] = total[leaf].astype(out.dtype)

    @pl.when(z_have)
    def _():
        store(add_near(add_far(first)))

    @pl.when(jnp.logical_not(z_have))
    def _():
        store(add_far(add_near(first)))

    inner = jnp.logical_not(outer)
    sent = (
        (0, me >= 0, leaf_dev), (1, place_sub < sub - 1, leaf_dev), (2, place_sub > 0, leaf_dev),
        (3, z_send & outer, kept), (3, z_send & inner, relayed),
        (4, first_turn, leaf_dev), (4, second_turn, turned),
        (5, z_have & inner, leaf_dev - relayed), (5, z_have & outer, leaf_dev - kept), (6, skip_turn, leaf_dev - turned),
    )
    for number, condition, count in sent:
        if count == 0:
            continue

        @pl.when(condition)
        def _(number=number, count=count):
            pltpu.make_async_copy(
                src.at[:, pl.ds(0, points * count)], src.at[:, pl.ds(0, points * count)],
                sent_sem.at[0],
            ).wait()
    pltpu.make_async_copy(
        buf_a.at[pl.ds(0, block - 1)], buf_a.at[pl.ds(0, block - 1)], sent_sem.at[0]
    ).wait()
    pltpu.make_async_copy(
        buf6.at[pl.ds(0, block_count - 2)], buf6.at[pl.ds(0, block_count - 2)], sent_sem.at[0]
    ).wait()
    pair_copy.wait_send()
    q_copy.wait_send()


def shards(sizes, sources, leaf_basis, transfer, coupling, near_blocks, near_pattern, far_pattern):
    sub, devices = sizes
    leaf_dev, points, rank = leaf_basis.shape
    rhs = sources.shape[1]
    near = near_blocks.shape[1]
    block = 2 * sub
    block_count = devices // block
    top_count = block_count.bit_length() - 1
    vmem = pl.BlockSpec(memory_space=pltpu.VMEM)
    hbm = pl.BlockSpec(memory_space=pl.ANY)
    dma = pltpu.SemaphoreType.DMA
    result = pl.pallas_call(
        functools.partial(kernel, (sub, devices, leaf_dev, near)),
        out_shape=pltpu.VMEM((rhs, leaf_dev * points), BF),
        in_specs=[hbm] * 7,
        out_specs=vmem,
        scratch_shapes=[
            pltpu.VMEM((5, leaf_dev, rhs, points // 2), BF),
            pltpu.VMEM((5, leaf_dev, rhs, points // 2), BF),
            pltpu.VMEM((leaf_dev, rank, points), BF),
            pltpu.VMEM((leaf_dev, near, points, points), BF),
            pltpu.VMEM((leaf_dev, rhs, 2 * rank), BF),
            pltpu.VMEM((block, rhs, 2 * rank), BF),
            pltpu.VMEM((2, 2, rhs, 2 * rank), BF),
            pltpu.VMEM((4, rhs, 2 * rank), BF),
            pltpu.VMEM((4, rhs, 2 * rank), BF),
            pltpu.VMEM((2 * block_count, rhs, 2 * rank), BF),
            pltpu.VMEM((2, 2 * rank, 2 * rank), BF),
            pltpu.VMEM((2 * top_count * rank, 2 * rank * leaf_dev), BF),
            pltpu.VMEM(transfer.shape, F32),
            pltpu.VMEM(coupling.shape, F32),
            pltpu.SMEM(near_pattern.shape[::-1], jnp.int32),
            pltpu.SMEM(far_pattern.shape[::-1], jnp.int32),
            dma((4,)),
            dma((1,)),
            dma((2, 2)),
            dma((leaf_dev,)),
            dma((leaf_dev // 2 + 1,)),
            dma((2,)),
            dma((3,)),
            pltpu.SemaphoreType.REGULAR((max(block_count - 2, 1), 2)),
        ],
        compiler_params=pltpu.CompilerParams(collective_id=0, has_side_effects=True),
    )(
        sources.T,
        leaf_basis.transpose(0, 2, 1),
        transfer,
        coupling,
        near_blocks,
        near_pattern.T,
        far_pattern.T,
    )
    return result.T


def solution(mesh):
    placed = (
        P(("leaf", "sub"), None),
        P(("leaf", "sub"), None, None),
        P(),
        P(),
        P(("leaf", "sub"), None, None, None),
        P(("leaf", "sub"), None),
        P(),
    )
    sizes = (mesh.shape["sub"], mesh.shape["leaf"] * mesh.shape["sub"])
    return jax.shard_map(
        functools.partial(shards, sizes),
        mesh=mesh, in_specs=placed, out_specs=P(("leaf", "sub"), None), check_vma=False,
    )
```

```python
import functools
from contextlib import nullcontext

import jax
import jax.numpy as jnp
from jax import lax
from jax.experimental import pallas as pl
from jax.experimental.pallas import tpu as pltpu
from jax.sharding import PartitionSpec as P

BF = jnp.bfloat16
F32 = jnp.float32
MESH = pl.DeviceIdType.MESH
PLACE_ONE = (0, 1, 2, 3, 3, 4, 5, 6)
PLACE_TWO = (6, 7, 8, 9, 10, 10, 10, 10)
PLACE_INNER = (6, 7, 8, 9, 10, 10, 10, 10)


def mark(name):
    return nullcontext()


def halves(x):
    hi = x.astype(BF)
    return hi, (x - hi.astype(F32)).astype(BF)


def split(x):
    return jnp.concatenate(halves(x), axis=1)


def nt(a, b):
    return lax.dot_general(a, b, (((1,), (1,)), ((), ())), preferred_element_type=F32)


def nn(a, b):
    return jnp.dot(a, b, preferred_element_type=F32)


def fold(y, width):
    return y[:, :width] + y[:, width:]


def relay_plan(leaves, turned, relayed):
    outer = [[] for _ in range(12)]
    inner = [[] for _ in range(12)]
    for leaf in range(leaves):
        outer[PLACE_ONE[leaf * 8 // leaves]].append((0, leaf))
    for leaf in range(turned):
        outer[PLACE_TWO[leaf * 8 // leaves]].append((1, leaf))
    for leaf in range(relayed):
        inner[PLACE_INNER[leaf * 8 // leaves]].append(leaf)
    return outer, inner


def kernel(
    cfg, src, basis, transfer_hbm, coupling_hbm, blocks, near_hbm, far_hbm, out,
    buf_lo, buf_hi, bas, nb, moment, buf_a, pair2, buf4, buf5, buf6, wdown, wpath, transfer, coupling,
    near_pat, far_pat, load_sem, sent_sem, near_recv, y_recv, z_recv, a_recv, far_recv, known, told,
):
    sub, devices, leaf_dev, near = cfg
    rank = basis.shape[1]
    rhs = src.shape[0]
    points = basis.shape[2]
    block = 2 * sub
    block_count = devices // block
    me = lax.axis_index("leaf") * sub + lax.axis_index("sub")
    mine = lax.rem(me, block)
    own_block = me // block
    place_sub = lax.rem(me, sub)
    upper = mine // sub
    has_prev = own_block > 0
    has_next = own_block < block_count - 1
    first_sub, last_sub = place_sub == 0, place_sub == sub - 1
    outer = first_sub | last_sub
    lower = upper == 0
    reach = sub // 2
    early = lower & (place_sub < reach)
    corner = jnp.logical_not(lower) & (place_sub >= reach)
    guide = lower & (place_sub >= reach)
    relayed = leaf_dev // 8
    kept = leaf_dev
    turned = leaf_dev // 2
    head = leaf_dev // 4

    y_slot = 4 - 4 * upper
    z_slot = 4 * upper
    across = me + sub - 2 * sub * upper
    z_step = block - 2 * block * upper
    z_target = me + z_step
    z_send = (lower & has_next) | (jnp.logical_not(lower) & has_prev)
    z_have = (lower & has_prev) | (jnp.logical_not(lower) & has_next)
    beyond = me - sub + 2 * sub * upper
    first_turn = (lower & first_sub) | (jnp.logical_not(lower) & last_sub)
    other_turn = (lower & last_sub) | (jnp.logical_not(lower) & first_sub)
    second_turn = z_have & other_turn
    skip_turn = z_send & other_turn
    skip_target = z_target + (sub - 1) * (2 * upper - 1)
    skip_source = me - (z_step + (sub - 1) * (2 * upper - 1))

    def target(dev):
        return (dev // sub, lax.rem(dev, sub))

    def remote(source, dest, send, recv, dev):
        return pltpu.make_async_remote_copy(
            src_ref=source, dst_ref=dest, send_sem=send, recv_sem=recv,
            device_id=target(dev), device_id_type=MESH,
        )

    barrier = pltpu.get_barrier_semaphore()
    peers = []
    for k in range(1, block):
        peers.append(own_block * block + lax.rem(mine + k, block))

    def greet(semaphore, condition, peer):
        @pl.when(condition)
        def _():
            pl.semaphore_signal(semaphore, inc=1, device_id=target(peer), device_id_type=MESH)

    expected = len(peers) - jnp.where(early, reach, 0) + sum(
        jnp.where(condition, 1, 0) for condition in (has_prev, has_next, z_have, skip_turn)
    )
    for peer in peers:
        place = lax.rem(peer, block)
        greet(barrier, jnp.logical_not(corner & (place < reach)), peer)
    greet(barrier, has_prev, me - block)
    greet(barrier, has_next, me + block)
    greet(barrier, z_have, beyond)
    greet(barrier, z_have & first_turn, skip_source)

    first_load = pltpu.make_async_copy(transfer_hbm, transfer, load_sem.at[0])
    base_load = pltpu.make_async_copy(basis, bas, load_sem.at[1])
    first_load.start()
    base_load.start()
    small_loads = [
        pltpu.make_async_copy(coupling_hbm, coupling, load_sem.at[1]),
        pltpu.make_async_copy(near_hbm, near_pat, load_sem.at[2]),
        pltpu.make_async_copy(far_hbm, far_pat, load_sem.at[3]),
    ]
    bufs = (buf_lo, buf_hi)
    short = points // 2
    middle_leaf = leaf_dev // 2

    def piece(slot, number):
        return bufs[number // middle_leaf].at[slot, pl.ds(2 * (number % middle_leaf), 2)]

    for half in range(2):
        for leaf in range(leaf_dev):
            pltpu.make_async_copy(
                src.at[:, pl.ds(points * leaf + short * half, short)], bufs[half].at[2, leaf],
                load_sem.at[2 + half],
            ).start()

    rounds = block_count - 2

    def make_known(r):
        greet(known.at[r - 1, 0], (own_block > 0) & (own_block + r < block_count), me - block)
        greet(known.at[r - 1, 1], (own_block < block_count - 1) & (own_block >= r), me + block)

    def get_known(r):
        @pl.when(own_block + r + 1 < block_count)
        def _():
            pl.semaphore_wait(known.at[r - 1, 0], 1)

        @pl.when(own_block >= r + 1)
        def _():
            pl.semaphore_wait(known.at[r - 1, 1], 1)

    def doubled(parts):
        rows = []
        for part in parts:
            row = split(part)
            rows += [row, row]
        return jnp.concatenate(rows, axis=0)

    with mark("00tc"):
        first_load.wait()
    sides = [transfer[side] for side in range(2)]
    step_weight = jnp.concatenate([doubled([side]) for side in sides], axis=1)
    w_up = {2: doubled(sides)}
    paths = sides
    while len(paths) < max(leaf_dev, block):
        wide = nn(split(jnp.concatenate(paths, axis=0)), step_weight)
        longer = jnp.concatenate(
            [fold(wide[:, : 2 * rank], rank), fold(wide[:, 2 * rank :], rank)], axis=0
        )
        paths = [longer[p * rank : (p + 1) * rank] for p in range(2 * len(paths))]
        w_up[len(paths)] = doubled(paths)

    def lift(parts, span):
        rows = [
            jnp.concatenate(parts[p * span : (p + 1) * span], axis=1)
            for p in range(len(parts) // span)
        ]
        rows = rows[0] if len(rows) == 1 else jnp.concatenate(rows, axis=0)
        lifted = split(fold(nn(rows, w_up[span]), rank))
        return [lifted[p * rhs : (p + 1) * rhs] for p in range(len(parts) // span)]

    def joined(leaf):
        return jnp.concatenate([buf_lo[2, leaf], buf_hi[2, leaf]], axis=1)

    def send_across(leaves):
        for leaf in leaves:
            remote(
                piece(2, leaf), piece(z_slot, leaf),
                sent_sem.at[0], y_recv.at[leaf], across,
            ).start()

    def send_beyond(leaves):
        for leaf in leaves:
            remote(
                piece(2, leaf), piece(y_slot, leaf),
                sent_sem.at[0], z_recv.at[min(leaf, turned)], beyond,
            ).start()

    with mark("01src"):
        for half in range(2):
            pltpu.make_async_copy(
                bufs[half].at[2], bufs[half].at[2], load_sem.at[2 + half]
            ).wait()
        base_load.wait()
    for copy in small_loads:
        copy.start()

    def find_moments():
        parts = [split(nt(joined(leaf), bas[leaf])) for leaf in range(leaf_dev)]
        for leaf in range(leaf_dev):
            moment[leaf] = parts[leaf]
        buf_a[mine] = lift(parts, leaf_dev)[0]

    with mark("02early"):
        pl.when(early & jnp.logical_not(has_prev))(find_moments)
    with mark("03barrier"):
        pl.semaphore_wait(barrier, expected)
    greet(told.at[0], guide, me - reach)
    pl.when(outer)(functools.partial(send_across, range(head)))
    with mark("02mom"):
        pl.when(jnp.logical_not(early & jnp.logical_not(has_prev)))(find_moments)
    with mark("04asend"):
        for k in [*range(2, block - 2, 2), 1, block - 2]:
            if k == block - 2:
                @pl.when(early)
                def _():
                    pl.semaphore_wait(told.at[0], 1)

            remote(
                buf_a.at[mine], buf_a.at[mine], sent_sem.at[0], a_recv.at[1 if k == 1 else 0],
                own_block * block + (mine ^ k),
            ).start()

    if rounds > 0:
        make_known(1)

    pl.when(outer)(functools.partial(send_across, range(head, leaf_dev)))
    for number, step in enumerate((1, -1)):
        @pl.when(place_sub < sub - 1 if step > 0 else place_sub > 0)
        def _(number=number, step=step):
            for leaf in range(leaf_dev):
                remote(
                    piece(2, leaf), piece(2 - step, leaf),
                    sent_sem.at[0], near_recv.at[number, leaf // middle_leaf], me + step,
                ).start()

    near_loads = [
        pltpu.make_async_copy(blocks.at[leaf], nb.at[leaf], load_sem.at[0])
        for leaf in range(leaf_dev)
    ]
    for copy in near_loads:
        copy.start()

    moment0 = [moment[leaf] for leaf in range(leaf_dev)]
    two = lift(moment0, leaf_dev // 2)
    pair2[0, 0] = two[0]
    pair2[0, 1] = two[1]
    pair_copy = remote(
        pair2.at[0], pair2.at[1], sent_sem.at[0], far_recv.at[0], me + 1 - 2 * lax.rem(me, 2)
    )
    pair_copy.start()

    def turn(slot, leaf):
        @pl.when(place_sub == 0)
        def _():
            remote(
                piece(slot, leaf), piece(3, leaf),
                sent_sem.at[0], near_recv.at[1, leaf // middle_leaf], me + sub - 1,
            ).start()

        @pl.when(place_sub == sub - 1)
        def _():
            remote(
                piece(slot, leaf), piece(1, leaf),
                sent_sem.at[0], near_recv.at[0, leaf // middle_leaf], me - sub + 1,
            ).start()

    def y_wait(leaf):
        remote(
            piece(y_slot, leaf), piece(y_slot, leaf), sent_sem.at[0], y_recv.at[leaf], across
        ).wait_recv()

    def relay_first(leaf):
        with mark(f"y{leaf}"):
            y_wait(leaf)

        if leaf < kept:
            @pl.when(z_send)
            def _():
                remote(
                    piece(y_slot, leaf), piece(z_slot, leaf),
                    sent_sem.at[0], z_recv.at[min(leaf, turned)], z_target,
                ).start()

        @pl.when(first_turn)
        def _():
            turn(y_slot, leaf)

        if leaf >= turned:
            @pl.when(skip_turn & first_sub)
            def _():
                remote(
                    piece(y_slot, leaf), piece(3, leaf),
                    sent_sem.at[0], near_recv.at[1, leaf // middle_leaf], skip_target,
                ).start()

            @pl.when(skip_turn & last_sub)
            def _():
                remote(
                    piece(y_slot, leaf), piece(1, leaf),
                    sent_sem.at[0], near_recv.at[0, leaf // middle_leaf], skip_target,
                ).start()

    def z_wait(leaf):
        remote(
            piece(z_slot, leaf), piece(z_slot, leaf), sent_sem.at[0], z_recv.at[leaf], across
        ).wait_recv()

    def relay_second(leaf):
        @pl.when(second_turn)
        def _():
            with mark(f"z{leaf}"):
                z_wait(leaf)
            turn(z_slot, leaf)

    row_starts = [0]
    size = leaf_dev * devices
    while size > 4:
        row_starts.append(row_starts[-1] + size)
        size //= 2

    def weight(offset, row):
        return jnp.full((rhs, 2 * rank), far_pat[offset, row].astype(F32), F32).astype(BF)

    for copy in small_loads:
        copy.wait()
    c_hi, c_lo = [], []
    for offset in range(3):
        hi, lo = halves(coupling[offset])
        c_hi += [hi, hi]
        c_lo += [lo, lo]
    w_couple = jnp.concatenate(
        [jnp.concatenate(c_hi, axis=1), jnp.concatenate(c_lo, axis=1)], axis=0
    )

    def couple(groups, rows):
        stacked = [
            jnp.concatenate(
                [weight(offset, row) * members[offset] for offset in range(3)], axis=1
            )
            for members, row in zip(groups, rows)
        ]
        stacked = stacked[0] if len(stacked) == 1 else jnp.concatenate(stacked, axis=0)
        return fold(nt(stacked, w_couple), rank)

    for side in range(2):
        hi, lo = halves(sides[side])
        wdown[side] = jnp.concatenate(
            [jnp.concatenate([hi, hi], axis=1), jnp.concatenate([lo, lo], axis=1)], axis=0
        )
    w_down = jnp.concatenate([wdown[0], wdown[1]], axis=0)
    def descend(field, step):
        return fold(nt(split(field), wdown[lax.rem(me >> step, 2)]), rank)

    def fan_out(field, rows):
        both = nt(split(field), w_down)
        children = []
        for p in range(field.shape[0] // rows):
            row = both[p * rows : (p + 1) * rows]
            children.append(fold(row[:, : 2 * rank], rank))
            children.append(fold(row[:, 2 * rank :], rank))
        return jnp.concatenate(children, axis=0)

    low_levels = leaf_dev.bit_length() - 1
    top_count = len(row_starts) - low_levels - 2
    eye = (
        lax.broadcasted_iota(jnp.int32, (rank, rank), 0)
        == lax.broadcasted_iota(jnp.int32, (rank, rank), 1)
    ).astype(F32)
    chain = eye
    for step in range(top_count, -1, -1):
        if step <= 1:
            chain = descend(chain, step)
        elif step < top_count + 1:
            chain = jnp.concatenate([descend(chain, step), eye], axis=0)
    for _ in range(low_levels):
        chain = fan_out(chain, top_count * rank)
    for leaf in range(leaf_dev):
        for number in range(top_count):
            begin = (leaf * top_count + number) * rank
            both = split(chain[begin : begin + rank])
            for half in range(2):
                wpath[
                    (2 * number + half) * rank : (2 * number + half + 1) * rank,
                    2 * rank * leaf : 2 * rank * (leaf + 1),
                ] = both

    ones = [(relay_first, leaf) for leaf in range(leaf_dev)]
    twos = [(relay_second, leaf) for leaf in range(turned)]
    plan_outer, plan_inner = relay_plan(leaf_dev, turned, relayed)

    def relays(point):
        early = [ones[leaf] if kind == 0 else twos[leaf] for kind, leaf in plan_outer[point]]
        if early:
            @pl.when(outer)
            def _():
                for step, leaf in early:
                    step(leaf)

        late = plan_inner[point]
        if late:
            @pl.when(jnp.logical_not(outer))
            def _():
                for leaf in late:
                    relay_first(leaf)

    if rounds > 0:
        with mark("06known"):
            get_known(1)
        if rounds > 1:
            make_known(2)
    with mark("07p0"):
        relays(0)

    locals_low = []
    level_vals, level_id = moment0, 0
    while (leaf_dev >> level_id) >= 4:
        if level_id:
            level_vals = lift(level_vals, 2)
        count = leaf_dev >> level_id
        locals_low.append(
            couple(
                [
                    [level_vals[c // 4 * 4 + (c + offset) % 4] for offset in range(1, 4)]
                    for c in range(count)
                ],
                [row_starts[level_id] + me * count + c for c in range(count)],
            )
        )
        level_id += 1
        if level_id == 1:
            pl.when(jnp.logical_not(outer))(functools.partial(send_across, range(leaf_dev)))
            with mark("08p1"):
                relays(1)
    with mark("09arecv"):
        pltpu.make_async_copy(
            buf_a.at[pl.ds(0, block // 2 - 1)], buf_a.at[pl.ds(0, block // 2 - 1)],
            a_recv.at[0],
        ).wait()
    for k in range(2, block, 2):
        remote(
            buf_a.at[mine ^ k], buf_a.at[mine ^ k], sent_sem.at[0], a_recv.at[1], me ^ 1
        ).start()
    with mark("08p2"):
        relays(2)
    with mark("09brecv"):
        pltpu.make_async_copy(
            buf_a.at[pl.ds(0, block // 2)], buf_a.at[pl.ds(0, block // 2)], a_recv.at[1]
        ).wait()
    eight = [buf_a[p] for p in range(block)]
    buf6[own_block] = lift(eight, block)[0]
    with mark("10known"):
        for r in range(2, rounds + 1):
            get_known(r)
            if r < rounds:
                make_known(r + 1)
    with mark("10bsend"):
        for k in range(block_count - 1, 1, -1):
            remote(
                buf6.at[own_block], buf6.at[own_block], sent_sem.at[0], far_recv.at[1],
                (own_block ^ k) * block + mine,
            ).start()
    with mark("11p3"):
        relays(3)
    five = lift(eight, block // 2)
    for p in range(2):
        buf5[p] = five[p]
    q_copy = remote(
        buf5.at[pl.ds(0, 2)], buf5.at[pl.ds(2, 2)], sent_sem.at[0], far_recv.at[2],
        (own_block + 1 - 2 * lax.rem(own_block, 2)) * block + mine,
    )
    q_copy.start()
    pl.when(z_have & jnp.logical_not(outer))(
        functools.partial(send_beyond, range(relayed, leaf_dev))
    )
    if kept < leaf_dev:
        pl.when(z_have & outer)(functools.partial(send_beyond, range(kept, leaf_dev)))
    with mark("11p4"):
        relays(4)
    for p, part in enumerate(lift(eight, 2)):
        buf4[p] = part

    with mark("12pair"):
        pair_copy.wait_recv()
    members2 = two + [pair2[1, 0], pair2[1, 1]]
    groups = [[members2[(c + offset) % 4] for offset in range(1, 4)] for c in range(2)]
    rows = [row_starts[level_id] + me * 2 + c for c in range(2)]
    level_id += 1
    groups.append(
        [buf_a[upper * sub + lax.rem(place_sub + offset, 4)] for offset in range(1, 4)]
    )
    rows.append(row_starts[level_id] + me)
    groups.append([buf4[lax.rem(mine // 2 + offset, 4)] for offset in range(1, 4)])
    rows.append(row_starts[level_id + 1] + me // 2)
    with mark("13p5"):
        relays(5)
    middle = couple(groups, rows)
    locals_low.append(middle[: 2 * rhs])
    field = middle[2 * rhs : 3 * rhs] + descend(middle[3 * rhs :], 0)
    with mark("13p6"):
        relays(6)
    for step in range(len(locals_low) - 1, -1, -1):
        field = locals_low[step] + fan_out(field, rhs)
        with mark("13p7"):
            relays(7 + len(locals_low) - 1 - step)

    with mark("15nearload"):
        pltpu.make_async_copy(nb, nb, load_sem.at[0]).wait()
    with mark("16first"):
        first = [nt(joined(leaf), nb[leaf, 0]) for leaf in range(leaf_dev)]
    with mark("17p10"):
        relays(10)
    with mark("19qwait"):
        q_copy.wait_recv()
    buf6[own_block ^ 1] = lift([buf5[2], buf5[3]], 2)[0]

    def add_far(base):
        with mark("18brecv"):
            pltpu.make_async_copy(
                buf6.at[pl.ds(0, block_count - 2)], buf6.at[pl.ds(0, block_count - 2)], far_recv.at[1]
            ).wait()
        groups = [[buf5[lax.rem(upper + offset, 4)] for offset in range(1, 4)]]
        rows = [row_starts[level_id + 2] + me // sub]
        first_six = level_id + 3
        start, span, level = 0, block_count, first_six
        while True:
            own = own_block >> (level - first_six)
            groups.append(
                [
                    buf6[start + own // 4 * 4 + lax.rem(lax.rem(own, 4) + offset, 4)]
                    for offset in range(1, 4)
                ]
            )
            rows.append(row_starts[level] + own)
            if span <= 4:
                break
            for p, part in enumerate(lift([buf6[start + p] for p in range(span)], 2)):
                buf6[start + span + p] = part
            start, span, level = start + span, span // 2, level + 1
        groups, rows = groups[::-1], rows[::-1]
        with mark("20top"):
            top = split(couple(groups, rows))
            top = jnp.concatenate([top[p * rhs : (p + 1) * rhs] for p in range(top_count)], axis=1)
            spread = nn(top, wpath[...])
        partial = []
        for leaf in range(leaf_dev):
            whole = split(
                field[leaf * rhs : (leaf + 1) * rhs]
                + fold(spread[:, 2 * rank * leaf : 2 * rank * (leaf + 1)], rank)
            )
            twice = jnp.concatenate([bas[leaf], bas[leaf]], axis=0)
            partial.append(base[leaf] + nn(whole, twice))
        return partial

    def add_near(base):
        total = base
        for half in range(2):
            begin = half * middle_leaf
            group = range(begin, begin + middle_leaf)
            with mark(f"21wait{half}"):
                @pl.when(jnp.logical_not(outer))
                def _(group=group):
                    for leaf in group:
                        if leaf >= relayed:
                            y_wait(leaf)

                @pl.when(z_have & jnp.logical_not(second_turn))
                def _(group=group):
                    for leaf in group:
                        if leaf < turned:
                            z_wait(leaf)

                if half:
                    @pl.when(z_have)
                    def _():
                        count = leaf_dev - turned
                        pltpu.make_async_copy(
                            src.at[:, pl.ds(0, points * count)], src.at[:, pl.ds(0, points * count)],
                            z_recv.at[turned],
                        ).wait()

            with mark(f"22near{half}"):
                for number, step in enumerate((-1, 1)):
                    @pl.when(me > 0 if step < 0 else me < devices - 1)
                    def _(number=number, step=step, half=half):
                        pltpu.make_async_copy(
                            bufs[half].at[2 + step], bufs[half].at[2 + step],
                            near_recv.at[number, half],
                        ).wait()
            with mark(f"23sum{half}"):
                added = []
                for leaf in range(leaf_dev):
                    acc = total[leaf]
                    for s in range(1, near):
                        index = near_pat[s, leaf]
                        gap = index // leaf_dev - me
                        place = jnp.where(
                            gap == -sub, 0,
                            jnp.where(
                                gap == -1, 1,
                                jnp.where(gap == 0, 2, jnp.where(gap == 1, 3, 4)),
                            ),
                        )
                        acc = acc + nt(
                            bufs[half][place, lax.rem(index, leaf_dev)],
                            nb[leaf, s, :, short * half : short * (half + 1)],
                        )
                    added.append(acc)
                total = added
        return total

    def store(total):
        for leaf in range(leaf_dev):
            out[:, points * leaf : points * (leaf + 1)] = total[leaf].astype(out.dtype)

    @pl.when(z_have)
    def _():
        store(add_near(add_far(first)))

    @pl.when(jnp.logical_not(z_have))
    def _():
        store(add_far(add_near(first)))

    inner = jnp.logical_not(outer)
    sent = (
        (0, me >= 0, leaf_dev), (1, place_sub < sub - 1, leaf_dev), (2, place_sub > 0, leaf_dev),
        (3, z_send & outer, kept), (3, z_send & inner, relayed),
        (4, first_turn, leaf_dev), (4, second_turn, turned),
        (5, z_have & inner, leaf_dev - relayed), (5, z_have & outer, leaf_dev - kept), (6, skip_turn, leaf_dev - turned),
    )
    for number, condition, count in sent:
        if count == 0:
            continue

        @pl.when(condition)
        def _(number=number, count=count):
            pltpu.make_async_copy(
                src.at[:, pl.ds(0, points * count)], src.at[:, pl.ds(0, points * count)],
                sent_sem.at[0],
            ).wait()
    pltpu.make_async_copy(
        buf_a.at[pl.ds(0, block - 1)], buf_a.at[pl.ds(0, block - 1)], sent_sem.at[0]
    ).wait()
    pltpu.make_async_copy(
        buf6.at[pl.ds(0, block_count - 2)], buf6.at[pl.ds(0, block_count - 2)], sent_sem.at[0]
    ).wait()
    pair_copy.wait_send()
    q_copy.wait_send()


def shards(sizes, sources, leaf_basis, transfer, coupling, near_blocks, near_pattern, far_pattern):
    sub, devices = sizes
    leaf_dev, points, rank = leaf_basis.shape
    rhs = sources.shape[1]
    near = near_blocks.shape[1]
    block = 2 * sub
    block_count = devices // block
    top_count = block_count.bit_length() - 1
    vmem = pl.BlockSpec(memory_space=pltpu.VMEM)
    hbm = pl.BlockSpec(memory_space=pl.ANY)
    dma = pltpu.SemaphoreType.DMA
    result = pl.pallas_call(
        functools.partial(kernel, (sub, devices, leaf_dev, near)),
        out_shape=pltpu.VMEM((rhs, leaf_dev * points), BF),
        in_specs=[hbm] * 7,
        out_specs=vmem,
        scratch_shapes=[
            pltpu.VMEM((5, leaf_dev, rhs, points // 2), BF),
            pltpu.VMEM((5, leaf_dev, rhs, points // 2), BF),
            pltpu.VMEM((leaf_dev, rank, points), BF),
            pltpu.VMEM((leaf_dev, near, points, points), BF),
            pltpu.VMEM((leaf_dev, rhs, 2 * rank), BF),
            pltpu.VMEM((block, rhs, 2 * rank), BF),
            pltpu.VMEM((2, 2, rhs, 2 * rank), BF),
            pltpu.VMEM((4, rhs, 2 * rank), BF),
            pltpu.VMEM((4, rhs, 2 * rank), BF),
            pltpu.VMEM((2 * block_count, rhs, 2 * rank), BF),
            pltpu.VMEM((2, 2 * rank, 2 * rank), BF),
            pltpu.VMEM((2 * top_count * rank, 2 * rank * leaf_dev), BF),
            pltpu.VMEM(transfer.shape, F32),
            pltpu.VMEM(coupling.shape, F32),
            pltpu.SMEM(near_pattern.shape[::-1], jnp.int32),
            pltpu.SMEM(far_pattern.shape[::-1], jnp.int32),
            dma((4,)),
            dma((1,)),
            dma((2, 2)),
            dma((leaf_dev,)),
            dma((leaf_dev // 2 + 1,)),
            dma((2,)),
            dma((3,)),
            pltpu.SemaphoreType.REGULAR((max(block_count - 2, 1), 2)),
            pltpu.SemaphoreType.REGULAR((1,)),
        ],
        compiler_params=pltpu.CompilerParams(collective_id=0, has_side_effects=True),
    )(
        sources.T,
        leaf_basis.transpose(0, 2, 1),
        transfer,
        coupling,
        near_blocks,
        near_pattern.T,
        far_pattern.T,
    )
    return result.T


def solution(mesh):
    placed = (
        P(("leaf", "sub"), None),
        P(("leaf", "sub"), None, None),
        P(),
        P(),
        P(("leaf", "sub"), None, None, None),
        P(("leaf", "sub"), None),
        P(),
    )
    sizes = (mesh.shape["sub"], mesh.shape["leaf"] * mesh.shape["sub"])
    return jax.shard_map(
        functools.partial(shards, sizes),
        mesh=mesh, in_specs=placed, out_specs=P(("leaf", "sub"), None), check_vma=False,
    )
```

```python
import functools
from contextlib import nullcontext

import jax
import jax.numpy as jnp
from jax import lax
from jax.experimental import pallas as pl
from jax.experimental.pallas import tpu as pltpu
from jax.sharding import PartitionSpec as P

BF = jnp.bfloat16
F32 = jnp.float32
MESH = pl.DeviceIdType.MESH
PLACE_ONE = (0, 1, 2, 3, 3, 4, 5, 6)
PLACE_TWO = (6, 7, 8, 9, 10, 10, 10, 10)
PLACE_INNER = (6, 7, 8, 9, 10, 10, 10, 10)


def mark(name):
    return nullcontext()


def halves(x):
    hi = x.astype(BF)
    return hi, (x - hi.astype(F32)).astype(BF)


def split(x):
    return jnp.concatenate(halves(x), axis=1)


def nt(a, b):
    return lax.dot_general(a, b, (((1,), (1,)), ((), ())), preferred_element_type=F32)


def nn(a, b):
    return jnp.dot(a, b, preferred_element_type=F32)


def fold(y, width):
    return y[:, :width] + y[:, width:]


def relay_plan(leaves, turned, relayed):
    outer = [[] for _ in range(12)]
    inner = [[] for _ in range(12)]
    for leaf in range(leaves):
        outer[PLACE_ONE[leaf * 8 // leaves]].append((0, leaf))
    for leaf in range(turned):
        outer[PLACE_TWO[leaf * 8 // leaves]].append((1, leaf))
    for leaf in range(relayed):
        inner[PLACE_INNER[leaf * 8 // leaves]].append(leaf)
    return outer, inner


def kernel(
    cfg, src, basis, transfer_hbm, coupling_hbm, blocks, near_hbm, far_hbm, out,
    buf_lo, buf_hi, bas, nb, moment, buf_a, pair2, buf4, buf5, buf6, wdown, wpath, transfer, coupling,
    near_pat, far_pat, load_sem, sent_sem, near_recv, y_recv, z_recv, a_recv, far_recv, known, told,
):
    sub, devices, leaf_dev, near = cfg
    rank = basis.shape[1]
    rhs = src.shape[0]
    points = basis.shape[2]
    block = 2 * sub
    block_count = devices // block
    me = lax.axis_index("leaf") * sub + lax.axis_index("sub")
    mine = lax.rem(me, block)
    own_block = me // block
    place_sub = lax.rem(me, sub)
    upper = mine // sub
    has_prev = own_block > 0
    has_next = own_block < block_count - 1
    first_sub, last_sub = place_sub == 0, place_sub == sub - 1
    outer = first_sub | last_sub
    lower = upper == 0
    reach = sub // 2
    early = lower & (place_sub < reach)
    corner = jnp.logical_not(lower) & (place_sub >= reach)
    guide = lower & (place_sub >= reach)
    relayed = leaf_dev // 8
    kept = leaf_dev
    turned = leaf_dev // 2 + 1
    head = leaf_dev // 4

    y_slot = 4 - 4 * upper
    z_slot = 4 * upper
    across = me + sub - 2 * sub * upper
    z_step = block - 2 * block * upper
    z_target = me + z_step
    z_send = (lower & has_next) | (jnp.logical_not(lower) & has_prev)
    z_have = (lower & has_prev) | (jnp.logical_not(lower) & has_next)
    beyond = me - sub + 2 * sub * upper
    first_turn = (lower & first_sub) | (jnp.logical_not(lower) & last_sub)
    other_turn = (lower & last_sub) | (jnp.logical_not(lower) & first_sub)
    second_turn = z_have & other_turn
    skip_turn = z_send & other_turn
    skip_target = z_target + (sub - 1) * (2 * upper - 1)
    skip_source = me - (z_step + (sub - 1) * (2 * upper - 1))

    def target(dev):
        return (dev // sub, lax.rem(dev, sub))

    def remote(source, dest, send, recv, dev):
        return pltpu.make_async_remote_copy(
            src_ref=source, dst_ref=dest, send_sem=send, recv_sem=recv,
            device_id=target(dev), device_id_type=MESH,
        )

    barrier = pltpu.get_barrier_semaphore()
    peers = []
    for k in range(1, block):
        peers.append(own_block * block + lax.rem(mine + k, block))

    def greet(semaphore, condition, peer):
        @pl.when(condition)
        def _():
            pl.semaphore_signal(semaphore, inc=1, device_id=target(peer), device_id_type=MESH)

    expected = len(peers) - jnp.where(early, reach, 0) + sum(
        jnp.where(condition, 1, 0) for condition in (has_prev, has_next, z_have, skip_turn)
    )
    for peer in peers:
        place = lax.rem(peer, block)
        greet(barrier, jnp.logical_not(corner & (place < reach)), peer)
    greet(barrier, has_prev, me - block)
    greet(barrier, has_next, me + block)
    greet(barrier, z_have, beyond)
    greet(barrier, z_have & first_turn, skip_source)

    first_load = pltpu.make_async_copy(transfer_hbm, transfer, load_sem.at[0])
    base_load = pltpu.make_async_copy(basis, bas, load_sem.at[1])
    first_load.start()
    base_load.start()
    small_loads = [
        pltpu.make_async_copy(coupling_hbm, coupling, load_sem.at[1]),
        pltpu.make_async_copy(near_hbm, near_pat, load_sem.at[2]),
        pltpu.make_async_copy(far_hbm, far_pat, load_sem.at[3]),
    ]
    bufs = (buf_lo, buf_hi)
    short = points // 2
    middle_leaf = leaf_dev // 2

    def piece(slot, number):
        return bufs[number // middle_leaf].at[slot, pl.ds(2 * (number % middle_leaf), 2)]

    for half in range(2):
        for leaf in range(leaf_dev):
            pltpu.make_async_copy(
                src.at[:, pl.ds(points * leaf + short * half, short)], bufs[half].at[2, leaf],
                load_sem.at[2 + half],
            ).start()

    rounds = block_count - 2

    def make_known(r):
        greet(known.at[r - 1, 0], (own_block > 0) & (own_block + r < block_count), me - block)
        greet(known.at[r - 1, 1], (own_block < block_count - 1) & (own_block >= r), me + block)

    def get_known(r):
        @pl.when(own_block + r + 1 < block_count)
        def _():
            pl.semaphore_wait(known.at[r - 1, 0], 1)

        @pl.when(own_block >= r + 1)
        def _():
            pl.semaphore_wait(known.at[r - 1, 1], 1)

    def doubled(parts):
        rows = []
        for part in parts:
            row = split(part)
            rows += [row, row]
        return jnp.concatenate(rows, axis=0)

    with mark("00tc"):
        first_load.wait()
    sides = [transfer[side] for side in range(2)]
    step_weight = jnp.concatenate([doubled([side]) for side in sides], axis=1)
    w_up = {2: doubled(sides)}
    paths = sides
    while len(paths) < max(leaf_dev, block):
        wide = nn(split(jnp.concatenate(paths, axis=0)), step_weight)
        longer = jnp.concatenate(
            [fold(wide[:, : 2 * rank], rank), fold(wide[:, 2 * rank :], rank)], axis=0
        )
        paths = [longer[p * rank : (p + 1) * rank] for p in range(2 * len(paths))]
        w_up[len(paths)] = doubled(paths)

    def lift(parts, span):
        rows = [
            jnp.concatenate(parts[p * span : (p + 1) * span], axis=1)
            for p in range(len(parts) // span)
        ]
        rows = rows[0] if len(rows) == 1 else jnp.concatenate(rows, axis=0)
        lifted = split(fold(nn(rows, w_up[span]), rank))
        return [lifted[p * rhs : (p + 1) * rhs] for p in range(len(parts) // span)]

    def joined(leaf):
        return jnp.concatenate([buf_lo[2, leaf], buf_hi[2, leaf]], axis=1)

    def send_across(leaves):
        for leaf in leaves:
            remote(
                piece(2, leaf), piece(z_slot, leaf),
                sent_sem.at[0], y_recv.at[leaf], across,
            ).start()

    def send_beyond(leaves):
        for leaf in leaves:
            remote(
                piece(2, leaf), piece(y_slot, leaf),
                sent_sem.at[0], z_recv.at[min(leaf, turned)], beyond,
            ).start()

    with mark("01src"):
        for half in range(2):
            pltpu.make_async_copy(
                bufs[half].at[2], bufs[half].at[2], load_sem.at[2 + half]
            ).wait()
        base_load.wait()
    for copy in small_loads:
        copy.start()

    def find_moments():
        parts = [split(nt(joined(leaf), bas[leaf])) for leaf in range(leaf_dev)]
        for leaf in range(leaf_dev):
            moment[leaf] = parts[leaf]
        buf_a[mine] = lift(parts, leaf_dev)[0]

    with mark("02early"):
        pl.when(early & jnp.logical_not(has_prev))(find_moments)
    with mark("03barrier"):
        pl.semaphore_wait(barrier, expected)
    greet(told.at[0], guide, me - reach)
    pl.when(outer)(functools.partial(send_across, range(head)))
    with mark("02mom"):
        pl.when(jnp.logical_not(early & jnp.logical_not(has_prev)))(find_moments)
    with mark("04asend"):
        for k in [*range(2, block - 2, 2), 1, block - 2]:
            if k == block - 2:
                @pl.when(early)
                def _():
                    pl.semaphore_wait(told.at[0], 1)

            remote(
                buf_a.at[mine], buf_a.at[mine], sent_sem.at[0], a_recv.at[1 if k == 1 else 0],
                own_block * block + (mine ^ k),
            ).start()

    if rounds > 0:
        make_known(1)

    pl.when(outer)(functools.partial(send_across, range(head, leaf_dev)))
    for number, step in enumerate((1, -1)):
        @pl.when(place_sub < sub - 1 if step > 0 else place_sub > 0)
        def _(number=number, step=step):
            for leaf in range(leaf_dev):
                remote(
                    piece(2, leaf), piece(2 - step, leaf),
                    sent_sem.at[0], near_recv.at[number, leaf // middle_leaf], me + step,
                ).start()

    near_loads = [
        pltpu.make_async_copy(blocks.at[leaf], nb.at[leaf], load_sem.at[0])
        for leaf in range(leaf_dev)
    ]
    for copy in near_loads:
        copy.start()

    moment0 = [moment[leaf] for leaf in range(leaf_dev)]
    two = lift(moment0, leaf_dev // 2)
    pair2[0, 0] = two[0]
    pair2[0, 1] = two[1]
    pair_copy = remote(
        pair2.at[0], pair2.at[1], sent_sem.at[0], far_recv.at[0], me + 1 - 2 * lax.rem(me, 2)
    )
    pair_copy.start()

    def turn(slot, leaf):
        @pl.when(place_sub == 0)
        def _():
            remote(
                piece(slot, leaf), piece(3, leaf),
                sent_sem.at[0], near_recv.at[1, leaf // middle_leaf], me + sub - 1,
            ).start()

        @pl.when(place_sub == sub - 1)
        def _():
            remote(
                piece(slot, leaf), piece(1, leaf),
                sent_sem.at[0], near_recv.at[0, leaf // middle_leaf], me - sub + 1,
            ).start()

    def y_wait(leaf):
        remote(
            piece(y_slot, leaf), piece(y_slot, leaf), sent_sem.at[0], y_recv.at[leaf], across
        ).wait_recv()

    def relay_first(leaf):
        with mark(f"y{leaf}"):
            y_wait(leaf)

        if leaf < kept:
            @pl.when(z_send)
            def _():
                remote(
                    piece(y_slot, leaf), piece(z_slot, leaf),
                    sent_sem.at[0], z_recv.at[min(leaf, turned)], z_target,
                ).start()

        @pl.when(first_turn)
        def _():
            turn(y_slot, leaf)

        if leaf >= turned:
            @pl.when(skip_turn & first_sub)
            def _():
                remote(
                    piece(y_slot, leaf), piece(3, leaf),
                    sent_sem.at[0], near_recv.at[1, leaf // middle_leaf], skip_target,
                ).start()

            @pl.when(skip_turn & last_sub)
            def _():
                remote(
                    piece(y_slot, leaf), piece(1, leaf),
                    sent_sem.at[0], near_recv.at[0, leaf // middle_leaf], skip_target,
                ).start()

    def z_wait(leaf):
        remote(
            piece(z_slot, leaf), piece(z_slot, leaf), sent_sem.at[0], z_recv.at[leaf], across
        ).wait_recv()

    def relay_second(leaf):
        @pl.when(second_turn)
        def _():
            with mark(f"z{leaf}"):
                z_wait(leaf)
            turn(z_slot, leaf)

    row_starts = [0]
    size = leaf_dev * devices
    while size > 4:
        row_starts.append(row_starts[-1] + size)
        size //= 2

    def weight(offset, row):
        return jnp.full((rhs, 2 * rank), far_pat[offset, row].astype(F32), F32).astype(BF)

    for copy in small_loads:
        copy.wait()
    c_hi, c_lo = [], []
    for offset in range(3):
        hi, lo = halves(coupling[offset])
        c_hi += [hi, hi]
        c_lo += [lo, lo]
    w_couple = jnp.concatenate(
        [jnp.concatenate(c_hi, axis=1), jnp.concatenate(c_lo, axis=1)], axis=0
    )

    def couple(groups, rows):
        stacked = [
            jnp.concatenate(
                [weight(offset, row) * members[offset] for offset in range(3)], axis=1
            )
            for members, row in zip(groups, rows)
        ]
        stacked = stacked[0] if len(stacked) == 1 else jnp.concatenate(stacked, axis=0)
        return fold(nt(stacked, w_couple), rank)

    for side in range(2):
        hi, lo = halves(sides[side])
        wdown[side] = jnp.concatenate(
            [jnp.concatenate([hi, hi], axis=1), jnp.concatenate([lo, lo], axis=1)], axis=0
        )
    w_down = jnp.concatenate([wdown[0], wdown[1]], axis=0)
    def descend(field, step):
        return fold(nt(split(field), wdown[lax.rem(me >> step, 2)]), rank)

    def fan_out(field, rows):
        both = nt(split(field), w_down)
        children = []
        for p in range(field.shape[0] // rows):
            row = both[p * rows : (p + 1) * rows]
            children.append(fold(row[:, : 2 * rank], rank))
            children.append(fold(row[:, 2 * rank :], rank))
        return jnp.concatenate(children, axis=0)

    low_levels = leaf_dev.bit_length() - 1
    top_count = len(row_starts) - low_levels - 2
    eye = (
        lax.broadcasted_iota(jnp.int32, (rank, rank), 0)
        == lax.broadcasted_iota(jnp.int32, (rank, rank), 1)
    ).astype(F32)
    chain = eye
    for step in range(top_count, -1, -1):
        if step <= 1:
            chain = descend(chain, step)
        elif step < top_count + 1:
            chain = jnp.concatenate([descend(chain, step), eye], axis=0)
    for _ in range(low_levels):
        chain = fan_out(chain, top_count * rank)
    for leaf in range(leaf_dev):
        for number in range(top_count):
            begin = (leaf * top_count + number) * rank
            both = split(chain[begin : begin + rank])
            for half in range(2):
                wpath[
                    (2 * number + half) * rank : (2 * number + half + 1) * rank,
                    2 * rank * leaf : 2 * rank * (leaf + 1),
                ] = both

    ones = [(relay_first, leaf) for leaf in range(leaf_dev)]
    twos = [(relay_second, leaf) for leaf in range(turned)]
    plan_outer, plan_inner = relay_plan(leaf_dev, turned, relayed)

    def relays(point):
        early = [ones[leaf] if kind == 0 else twos[leaf] for kind, leaf in plan_outer[point]]
        if early:
            @pl.when(outer)
            def _():
                for step, leaf in early:
                    step(leaf)

        late = plan_inner[point]
        if late:
            @pl.when(jnp.logical_not(outer))
            def _():
                for leaf in late:
                    relay_first(leaf)

    if rounds > 0:
        with mark("06known"):
            get_known(1)
        if rounds > 1:
            make_known(2)
    with mark("07p0"):
        relays(0)

    locals_low = []
    level_vals, level_id = moment0, 0
    while (leaf_dev >> level_id) >= 4:
        if level_id:
            level_vals = lift(level_vals, 2)
        count = leaf_dev >> level_id
        locals_low.append(
            couple(
                [
                    [level_vals[c // 4 * 4 + (c + offset) % 4] for offset in range(1, 4)]
                    for c in range(count)
                ],
                [row_starts[level_id] + me * count + c for c in range(count)],
            )
        )
        level_id += 1
        if level_id == 1:
            pl.when(jnp.logical_not(outer))(functools.partial(send_across, range(leaf_dev)))
            with mark("08p1"):
                relays(1)
    with mark("09arecv"):
        pltpu.make_async_copy(
            buf_a.at[pl.ds(0, block // 2 - 1)], buf_a.at[pl.ds(0, block // 2 - 1)],
            a_recv.at[0],
        ).wait()
    for k in range(2, block, 2):
        remote(
            buf_a.at[mine ^ k], buf_a.at[mine ^ k], sent_sem.at[0], a_recv.at[1], me ^ 1
        ).start()
    with mark("08p2"):
        relays(2)
    pl.when(z_have & jnp.logical_not(outer))(
        functools.partial(send_beyond, range(relayed, 3))
    )
    with mark("09brecv"):
        pltpu.make_async_copy(
            buf_a.at[pl.ds(0, block // 2)], buf_a.at[pl.ds(0, block // 2)], a_recv.at[1]
        ).wait()
    eight = [buf_a[p] for p in range(block)]
    buf6[own_block] = lift(eight, block)[0]
    with mark("10known"):
        for r in range(2, rounds + 1):
            get_known(r)
            if r < rounds:
                make_known(r + 1)
    with mark("10bsend"):
        for k in range(block_count - 1, 1, -1):
            remote(
                buf6.at[own_block], buf6.at[own_block], sent_sem.at[0], far_recv.at[1],
                (own_block ^ k) * block + mine,
            ).start()
    with mark("11p3"):
        relays(3)
    five = lift(eight, block // 2)
    for p in range(2):
        buf5[p] = five[p]
    q_copy = remote(
        buf5.at[pl.ds(0, 2)], buf5.at[pl.ds(2, 2)], sent_sem.at[0], far_recv.at[2],
        (own_block + 1 - 2 * lax.rem(own_block, 2)) * block + mine,
    )
    q_copy.start()
    pl.when(z_have & jnp.logical_not(outer))(
        functools.partial(send_beyond, range(3, leaf_dev))
    )
    if kept < leaf_dev:
        pl.when(z_have & outer)(functools.partial(send_beyond, range(kept, leaf_dev)))
    with mark("11p4"):
        relays(4)
    for p, part in enumerate(lift(eight, 2)):
        buf4[p] = part

    with mark("12pair"):
        pair_copy.wait_recv()
    members2 = two + [pair2[1, 0], pair2[1, 1]]
    groups = [[members2[(c + offset) % 4] for offset in range(1, 4)] for c in range(2)]
    rows = [row_starts[level_id] + me * 2 + c for c in range(2)]
    level_id += 1
    groups.append(
        [buf_a[upper * sub + lax.rem(place_sub + offset, 4)] for offset in range(1, 4)]
    )
    rows.append(row_starts[level_id] + me)
    groups.append([buf4[lax.rem(mine // 2 + offset, 4)] for offset in range(1, 4)])
    rows.append(row_starts[level_id + 1] + me // 2)
    with mark("13p5"):
        relays(5)
    middle = couple(groups, rows)
    locals_low.append(middle[: 2 * rhs])
    field = middle[2 * rhs : 3 * rhs] + descend(middle[3 * rhs :], 0)
    with mark("13p6"):
        relays(6)
    for step in range(len(locals_low) - 1, -1, -1):
        field = locals_low[step] + fan_out(field, rhs)
        with mark("13p7"):
            relays(7 + len(locals_low) - 1 - step)

    with mark("15nearload"):
        pltpu.make_async_copy(nb, nb, load_sem.at[0]).wait()
    with mark("16first"):
        first = [nt(joined(leaf), nb[leaf, 0]) for leaf in range(leaf_dev)]
    with mark("17p10"):
        relays(10)
    with mark("19qwait"):
        q_copy.wait_recv()
    buf6[own_block ^ 1] = lift([buf5[2], buf5[3]], 2)[0]

    def add_far(base):
        with mark("18brecv"):
            pltpu.make_async_copy(
                buf6.at[pl.ds(0, block_count - 2)], buf6.at[pl.ds(0, block_count - 2)], far_recv.at[1]
            ).wait()
        groups = [[buf5[lax.rem(upper + offset, 4)] for offset in range(1, 4)]]
        rows = [row_starts[level_id + 2] + me // sub]
        first_six = level_id + 3
        start, span, level = 0, block_count, first_six
        while True:
            own = own_block >> (level - first_six)
            groups.append(
                [
                    buf6[start + own // 4 * 4 + lax.rem(lax.rem(own, 4) + offset, 4)]
                    for offset in range(1, 4)
                ]
            )
            rows.append(row_starts[level] + own)
            if span <= 4:
                break
            for p, part in enumerate(lift([buf6[start + p] for p in range(span)], 2)):
                buf6[start + span + p] = part
            start, span, level = start + span, span // 2, level + 1
        groups, rows = groups[::-1], rows[::-1]
        with mark("20top"):
            top = split(couple(groups, rows))
            top = jnp.concatenate([top[p * rhs : (p + 1) * rhs] for p in range(top_count)], axis=1)
            spread = nn(top, wpath[...])
        partial = []
        for leaf in range(leaf_dev):
            whole = split(
                field[leaf * rhs : (leaf + 1) * rhs]
                + fold(spread[:, 2 * rank * leaf : 2 * rank * (leaf + 1)], rank)
            )
            twice = jnp.concatenate([bas[leaf], bas[leaf]], axis=0)
            partial.append(base[leaf] + nn(whole, twice))
        return partial

    def add_near(base):
        total = base
        for half in range(2):
            begin = half * middle_leaf
            group = range(begin, begin + middle_leaf)
            with mark(f"21wait{half}"):
                @pl.when(jnp.logical_not(outer))
                def _(group=group):
                    for leaf in group:
                        if leaf >= relayed:
                            y_wait(leaf)

                @pl.when(z_have & jnp.logical_not(second_turn))
                def _(group=group):
                    for leaf in group:
                        if leaf < turned:
                            z_wait(leaf)

                if half:
                    @pl.when(z_have)
                    def _():
                        count = leaf_dev - turned
                        pltpu.make_async_copy(
                            src.at[:, pl.ds(0, points * count)], src.at[:, pl.ds(0, points * count)],
                            z_recv.at[turned],
                        ).wait()

            with mark(f"22near{half}"):
                for number, step in enumerate((-1, 1)):
                    @pl.when(me > 0 if step < 0 else me < devices - 1)
                    def _(number=number, step=step, half=half):
                        pltpu.make_async_copy(
                            bufs[half].at[2 + step], bufs[half].at[2 + step],
                            near_recv.at[number, half],
                        ).wait()
            with mark(f"23sum{half}"):
                added = []
                for leaf in range(leaf_dev):
                    acc = total[leaf]
                    for s in range(1, near):
                        index = near_pat[s, leaf]
                        gap = index // leaf_dev - me
                        place = jnp.where(
                            gap == -sub, 0,
                            jnp.where(
                                gap == -1, 1,
                                jnp.where(gap == 0, 2, jnp.where(gap == 1, 3, 4)),
                            ),
                        )
                        acc = acc + nt(
                            bufs[half][place, lax.rem(index, leaf_dev)],
                            nb[leaf, s, :, short * half : short * (half + 1)],
                        )
                    added.append(acc)
                total = added
        return total

    def store(total):
        for leaf in range(leaf_dev):
            out[:, points * leaf : points * (leaf + 1)] = total[leaf].astype(out.dtype)

    @pl.when(z_have)
    def _():
        store(add_near(add_far(first)))

    @pl.when(jnp.logical_not(z_have))
    def _():
        store(add_far(add_near(first)))

    inner = jnp.logical_not(outer)
    sent = (
        (0, me >= 0, leaf_dev), (1, place_sub < sub - 1, leaf_dev), (2, place_sub > 0, leaf_dev),
        (3, z_send & outer, kept), (3, z_send & inner, relayed),
        (4, first_turn, leaf_dev), (4, second_turn, turned),
        (5, z_have & inner, leaf_dev - relayed), (5, z_have & outer, leaf_dev - kept), (6, skip_turn, leaf_dev - turned),
    )
    for number, condition, count in sent:
        if count == 0:
            continue

        @pl.when(condition)
        def _(number=number, count=count):
            pltpu.make_async_copy(
                src.at[:, pl.ds(0, points * count)], src.at[:, pl.ds(0, points * count)],
                sent_sem.at[0],
            ).wait()
    pltpu.make_async_copy(
        buf_a.at[pl.ds(0, block - 1)], buf_a.at[pl.ds(0, block - 1)], sent_sem.at[0]
    ).wait()
    pltpu.make_async_copy(
        buf6.at[pl.ds(0, block_count - 2)], buf6.at[pl.ds(0, block_count - 2)], sent_sem.at[0]
    ).wait()
    pair_copy.wait_send()
    q_copy.wait_send()


def shards(sizes, sources, leaf_basis, transfer, coupling, near_blocks, near_pattern, far_pattern):
    sub, devices = sizes
    leaf_dev, points, rank = leaf_basis.shape
    rhs = sources.shape[1]
    near = near_blocks.shape[1]
    block = 2 * sub
    block_count = devices // block
    top_count = block_count.bit_length() - 1
    vmem = pl.BlockSpec(memory_space=pltpu.VMEM)
    hbm = pl.BlockSpec(memory_space=pl.ANY)
    dma = pltpu.SemaphoreType.DMA
    result = pl.pallas_call(
        functools.partial(kernel, (sub, devices, leaf_dev, near)),
        out_shape=pltpu.VMEM((rhs, leaf_dev * points), BF),
        in_specs=[hbm] * 7,
        out_specs=vmem,
        scratch_shapes=[
            pltpu.VMEM((5, leaf_dev, rhs, points // 2), BF),
            pltpu.VMEM((5, leaf_dev, rhs, points // 2), BF),
            pltpu.VMEM((leaf_dev, rank, points), BF),
            pltpu.VMEM((leaf_dev, near, points, points), BF),
            pltpu.VMEM((leaf_dev, rhs, 2 * rank), BF),
            pltpu.VMEM((block, rhs, 2 * rank), BF),
            pltpu.VMEM((2, 2, rhs, 2 * rank), BF),
            pltpu.VMEM((4, rhs, 2 * rank), BF),
            pltpu.VMEM((4, rhs, 2 * rank), BF),
            pltpu.VMEM((2 * block_count, rhs, 2 * rank), BF),
            pltpu.VMEM((2, 2 * rank, 2 * rank), BF),
            pltpu.VMEM((2 * top_count * rank, 2 * rank * leaf_dev), BF),
            pltpu.VMEM(transfer.shape, F32),
            pltpu.VMEM(coupling.shape, F32),
            pltpu.SMEM(near_pattern.shape[::-1], jnp.int32),
            pltpu.SMEM(far_pattern.shape[::-1], jnp.int32),
            dma((4,)),
            dma((1,)),
            dma((2, 2)),
            dma((leaf_dev,)),
            dma((leaf_dev // 2 + 2,)),
            dma((2,)),
            dma((3,)),
            pltpu.SemaphoreType.REGULAR((max(block_count - 2, 1), 2)),
            pltpu.SemaphoreType.REGULAR((1,)),
        ],
        compiler_params=pltpu.CompilerParams(collective_id=0, has_side_effects=True),
    )(
        sources.T,
        leaf_basis.transpose(0, 2, 1),
        transfer,
        coupling,
        near_blocks,
        near_pattern.T,
        far_pattern.T,
    )
    return result.T


def solution(mesh):
    placed = (
        P(("leaf", "sub"), None),
        P(("leaf", "sub"), None, None),
        P(),
        P(),
        P(("leaf", "sub"), None, None, None),
        P(("leaf", "sub"), None),
        P(),
    )
    sizes = (mesh.shape["sub"], mesh.shape["leaf"] * mesh.shape["sub"])
    return jax.shard_map(
        functools.partial(shards, sizes),
        mesh=mesh, in_specs=placed, out_specs=P(("leaf", "sub"), None), check_vma=False,
    )
```

```python
import functools
from contextlib import nullcontext

import jax
import jax.numpy as jnp
from jax import lax
from jax.experimental import pallas as pl
from jax.experimental.pallas import tpu as pltpu
from jax.sharding import PartitionSpec as P

BF = jnp.bfloat16
F32 = jnp.float32
MESH = pl.DeviceIdType.MESH
PLACE_EARLY = (1, 1, 2, 3, 4, 4, 5, 6)
PLACE_ONE = (0, 1, 2, 3, 3, 4, 5, 6)
PLACE_TWO = (6, 7, 8, 9, 10, 10, 10, 10)
PLACE_INNER = (6, 7, 8, 9, 10, 10, 10, 10)


def mark(name):
    return nullcontext()


def halves(x):
    hi = x.astype(BF)
    return hi, (x - hi.astype(F32)).astype(BF)


def split(x):
    return jnp.concatenate(halves(x), axis=1)


def nt(a, b):
    return lax.dot_general(a, b, (((1,), (1,)), ((), ())), preferred_element_type=F32)


def nn(a, b):
    return jnp.dot(a, b, preferred_element_type=F32)


def fold(y, width):
    return y[:, :width] + y[:, width:]


def relay_plan(leaves, turned, relayed):
    outer, soon, inner = ([[] for _ in range(12)] for _ in range(3))
    for leaf in range(leaves):
        outer[PLACE_ONE[leaf * 8 // leaves]].append((0, leaf))
        soon[PLACE_EARLY[leaf * 8 // leaves]].append((0, leaf))
    for leaf in range(turned):
        outer[PLACE_TWO[leaf * 8 // leaves]].append((1, leaf))
    for leaf in range(relayed):
        inner[PLACE_INNER[leaf * 8 // leaves]].append(leaf)
    return outer, soon, inner


def kernel(
    cfg, src, basis, transfer_hbm, coupling_hbm, blocks, near_hbm, far_hbm, out,
    buf_lo, buf_hi, bas, nb, moment, buf_a, pair2, buf4, buf5, buf6, wdown, wpath, transfer, coupling,
    near_pat, far_pat, load_sem, sent_sem, near_recv, y_recv, z_recv, a_recv, far_recv, known, told,
):
    sub, devices, leaf_dev, near = cfg
    rank = basis.shape[1]
    rhs = src.shape[0]
    points = basis.shape[2]
    block = 2 * sub
    block_count = devices // block
    me = lax.axis_index("leaf") * sub + lax.axis_index("sub")
    mine = lax.rem(me, block)
    own_block = me // block
    place_sub = lax.rem(me, sub)
    upper = mine // sub
    has_prev = own_block > 0
    has_next = own_block < block_count - 1
    first_sub, last_sub = place_sub == 0, place_sub == sub - 1
    outer = first_sub | last_sub
    lower = upper == 0
    reach = sub // 2
    early = lower & (place_sub < reach)
    corner = jnp.logical_not(lower) & (place_sub >= reach)
    guide = lower & (place_sub >= reach)
    relayed = leaf_dev // 8
    kept = leaf_dev
    turned = leaf_dev // 2 + 1
    head = leaf_dev // 4

    y_slot = 4 - 4 * upper
    z_slot = 4 * upper
    across = me + sub - 2 * sub * upper
    z_step = block - 2 * block * upper
    z_target = me + z_step
    z_send = (lower & has_next) | (jnp.logical_not(lower) & has_prev)
    z_have = (lower & has_prev) | (jnp.logical_not(lower) & has_next)
    beyond = me - sub + 2 * sub * upper
    first_turn = (lower & first_sub) | (jnp.logical_not(lower) & last_sub)
    other_turn = (lower & last_sub) | (jnp.logical_not(lower) & first_sub)
    second_turn = z_have & other_turn
    skip_turn = z_send & other_turn
    skip_target = z_target + (sub - 1) * (2 * upper - 1)
    skip_source = me - (z_step + (sub - 1) * (2 * upper - 1))

    def target(dev):
        return (dev // sub, lax.rem(dev, sub))

    def remote(source, dest, send, recv, dev):
        return pltpu.make_async_remote_copy(
            src_ref=source, dst_ref=dest, send_sem=send, recv_sem=recv,
            device_id=target(dev), device_id_type=MESH,
        )

    barrier = pltpu.get_barrier_semaphore()
    peers = []
    for k in range(1, block):
        peers.append(own_block * block + lax.rem(mine + k, block))

    def greet(semaphore, condition, peer):
        @pl.when(condition)
        def _():
            pl.semaphore_signal(semaphore, inc=1, device_id=target(peer), device_id_type=MESH)

    expected = len(peers) - jnp.where(early, reach, 0) + sum(
        jnp.where(condition, 1, 0) for condition in (has_prev, has_next, z_have, skip_turn)
    )
    for peer in peers:
        place = lax.rem(peer, block)
        greet(barrier, jnp.logical_not(corner & (place < reach)), peer)
    greet(barrier, has_prev, me - block)
    greet(barrier, has_next, me + block)
    greet(barrier, z_have, beyond)
    greet(barrier, z_have & first_turn, skip_source)

    first_load = pltpu.make_async_copy(transfer_hbm, transfer, load_sem.at[0])
    base_load = pltpu.make_async_copy(basis, bas, load_sem.at[1])
    first_load.start()
    base_load.start()
    small_loads = [
        pltpu.make_async_copy(coupling_hbm, coupling, load_sem.at[1]),
        pltpu.make_async_copy(near_hbm, near_pat, load_sem.at[2]),
        pltpu.make_async_copy(far_hbm, far_pat, load_sem.at[3]),
    ]
    bufs = (buf_lo, buf_hi)
    short = points // 2
    middle_leaf = leaf_dev // 2

    def piece(slot, number):
        return bufs[number // middle_leaf].at[slot, pl.ds(2 * (number % middle_leaf), 2)]

    for half in range(2):
        for leaf in range(leaf_dev):
            pltpu.make_async_copy(
                src.at[:, pl.ds(points * leaf + short * half, short)], bufs[half].at[2, leaf],
                load_sem.at[2 + half],
            ).start()

    rounds = block_count - 2

    def make_known(r):
        greet(known.at[r - 1, 0], (own_block > 0) & (own_block + r < block_count), me - block)
        greet(known.at[r - 1, 1], (own_block < block_count - 1) & (own_block >= r), me + block)

    def get_known(r):
        @pl.when(own_block + r + 1 < block_count)
        def _():
            pl.semaphore_wait(known.at[r - 1, 0], 1)

        @pl.when(own_block >= r + 1)
        def _():
            pl.semaphore_wait(known.at[r - 1, 1], 1)

    def doubled(parts):
        rows = []
        for part in parts:
            row = split(part)
            rows += [row, row]
        return jnp.concatenate(rows, axis=0)

    with mark("00tc"):
        first_load.wait()
    sides = [transfer[side] for side in range(2)]
    step_weight = jnp.concatenate([doubled([side]) for side in sides], axis=1)
    w_up = {2: doubled(sides)}
    paths = sides
    while len(paths) < max(leaf_dev, block):
        wide = nn(split(jnp.concatenate(paths, axis=0)), step_weight)
        longer = jnp.concatenate(
            [fold(wide[:, : 2 * rank], rank), fold(wide[:, 2 * rank :], rank)], axis=0
        )
        paths = [longer[p * rank : (p + 1) * rank] for p in range(2 * len(paths))]
        w_up[len(paths)] = doubled(paths)

    def lift(parts, span):
        rows = [
            jnp.concatenate(parts[p * span : (p + 1) * span], axis=1)
            for p in range(len(parts) // span)
        ]
        rows = rows[0] if len(rows) == 1 else jnp.concatenate(rows, axis=0)
        lifted = split(fold(nn(rows, w_up[span]), rank))
        return [lifted[p * rhs : (p + 1) * rhs] for p in range(len(parts) // span)]

    def joined(leaf):
        return jnp.concatenate([buf_lo[2, leaf], buf_hi[2, leaf]], axis=1)

    def send_across(leaves):
        for leaf in leaves:
            remote(
                piece(2, leaf), piece(z_slot, leaf),
                sent_sem.at[0], y_recv.at[leaf], across,
            ).start()

    def send_beyond(leaves):
        for leaf in leaves:
            remote(
                piece(2, leaf), piece(y_slot, leaf),
                sent_sem.at[0], z_recv.at[min(leaf, turned)], beyond,
            ).start()

    with mark("01src"):
        for half in range(2):
            pltpu.make_async_copy(
                bufs[half].at[2], bufs[half].at[2], load_sem.at[2 + half]
            ).wait()
        base_load.wait()
    for copy in small_loads:
        copy.start()

    def find_moments():
        parts = [split(nt(joined(leaf), bas[leaf])) for leaf in range(leaf_dev)]
        for leaf in range(leaf_dev):
            moment[leaf] = parts[leaf]
        buf_a[mine] = lift(parts, leaf_dev)[0]

    with mark("02early"):
        pl.when(early & jnp.logical_not(has_prev))(find_moments)
    with mark("03barrier"):
        pl.semaphore_wait(barrier, expected)
    greet(told.at[0], guide, me - reach)
    pl.when(outer)(functools.partial(send_across, range(head)))
    with mark("02mom"):
        pl.when(jnp.logical_not(early & jnp.logical_not(has_prev)))(find_moments)
    with mark("04asend"):
        for k in [*range(2, block - 2, 2), 1, block - 2]:
            if k == block - 2:
                @pl.when(early)
                def _():
                    pl.semaphore_wait(told.at[0], 1)

            remote(
                buf_a.at[mine], buf_a.at[mine], sent_sem.at[0], a_recv.at[1 if k == 1 else 0],
                own_block * block + (mine ^ k),
            ).start()

    if rounds > 0:
        make_known(1)

    pl.when(outer)(functools.partial(send_across, range(head, leaf_dev)))
    for number, step in enumerate((1, -1)):
        @pl.when(place_sub < sub - 1 if step > 0 else place_sub > 0)
        def _(number=number, step=step):
            for leaf in range(leaf_dev):
                remote(
                    piece(2, leaf), piece(2 - step, leaf),
                    sent_sem.at[0], near_recv.at[number, leaf // middle_leaf], me + step,
                ).start()

    near_loads = [
        pltpu.make_async_copy(blocks.at[leaf], nb.at[leaf], load_sem.at[0])
        for leaf in range(leaf_dev)
    ]
    for copy in near_loads:
        copy.start()

    moment0 = [moment[leaf] for leaf in range(leaf_dev)]
    two = lift(moment0, leaf_dev // 2)
    pair2[0, 0] = two[0]
    pair2[0, 1] = two[1]
    pair_copy = remote(
        pair2.at[0], pair2.at[1], sent_sem.at[0], far_recv.at[0], me + 1 - 2 * lax.rem(me, 2)
    )
    pair_copy.start()

    def turn(slot, leaf):
        @pl.when(place_sub == 0)
        def _():
            remote(
                piece(slot, leaf), piece(3, leaf),
                sent_sem.at[0], near_recv.at[1, leaf // middle_leaf], me + sub - 1,
            ).start()

        @pl.when(place_sub == sub - 1)
        def _():
            remote(
                piece(slot, leaf), piece(1, leaf),
                sent_sem.at[0], near_recv.at[0, leaf // middle_leaf], me - sub + 1,
            ).start()

    def y_wait(leaf):
        remote(
            piece(y_slot, leaf), piece(y_slot, leaf), sent_sem.at[0], y_recv.at[leaf], across
        ).wait_recv()

    def relay_first(leaf):
        with mark(f"y{leaf}"):
            y_wait(leaf)

        if leaf < kept:
            @pl.when(z_send)
            def _():
                remote(
                    piece(y_slot, leaf), piece(z_slot, leaf),
                    sent_sem.at[0], z_recv.at[min(leaf, turned)], z_target,
                ).start()

        @pl.when(first_turn)
        def _():
            turn(y_slot, leaf)

        if leaf >= turned:
            @pl.when(skip_turn & first_sub)
            def _():
                remote(
                    piece(y_slot, leaf), piece(3, leaf),
                    sent_sem.at[0], near_recv.at[1, leaf // middle_leaf], skip_target,
                ).start()

            @pl.when(skip_turn & last_sub)
            def _():
                remote(
                    piece(y_slot, leaf), piece(1, leaf),
                    sent_sem.at[0], near_recv.at[0, leaf // middle_leaf], skip_target,
                ).start()

    def z_wait(leaf):
        remote(
            piece(z_slot, leaf), piece(z_slot, leaf), sent_sem.at[0], z_recv.at[leaf], across
        ).wait_recv()

    def relay_second(leaf):
        @pl.when(second_turn)
        def _():
            with mark(f"z{leaf}"):
                z_wait(leaf)
            turn(z_slot, leaf)

    row_starts = [0]
    size = leaf_dev * devices
    while size > 4:
        row_starts.append(row_starts[-1] + size)
        size //= 2

    def weight(offset, row):
        return jnp.full((rhs, 2 * rank), far_pat[offset, row].astype(F32), F32).astype(BF)

    for copy in small_loads:
        copy.wait()
    c_hi, c_lo = [], []
    for offset in range(3):
        hi, lo = halves(coupling[offset])
        c_hi += [hi, hi]
        c_lo += [lo, lo]
    w_couple = jnp.concatenate(
        [jnp.concatenate(c_hi, axis=1), jnp.concatenate(c_lo, axis=1)], axis=0
    )

    def couple(groups, rows):
        stacked = [
            jnp.concatenate(
                [weight(offset, row) * members[offset] for offset in range(3)], axis=1
            )
            for members, row in zip(groups, rows)
        ]
        stacked = stacked[0] if len(stacked) == 1 else jnp.concatenate(stacked, axis=0)
        return fold(nt(stacked, w_couple), rank)

    for side in range(2):
        hi, lo = halves(sides[side])
        wdown[side] = jnp.concatenate(
            [jnp.concatenate([hi, hi], axis=1), jnp.concatenate([lo, lo], axis=1)], axis=0
        )
    w_down = jnp.concatenate([wdown[0], wdown[1]], axis=0)
    def descend(field, step):
        return fold(nt(split(field), wdown[lax.rem(me >> step, 2)]), rank)

    def fan_out(field, rows):
        both = nt(split(field), w_down)
        children = []
        for p in range(field.shape[0] // rows):
            row = both[p * rows : (p + 1) * rows]
            children.append(fold(row[:, : 2 * rank], rank))
            children.append(fold(row[:, 2 * rank :], rank))
        return jnp.concatenate(children, axis=0)

    low_levels = leaf_dev.bit_length() - 1
    top_count = len(row_starts) - low_levels - 2
    eye = (
        lax.broadcasted_iota(jnp.int32, (rank, rank), 0)
        == lax.broadcasted_iota(jnp.int32, (rank, rank), 1)
    ).astype(F32)
    chain = eye
    for step in range(top_count, -1, -1):
        if step <= 1:
            chain = descend(chain, step)
        elif step < top_count + 1:
            chain = jnp.concatenate([descend(chain, step), eye], axis=0)
    for _ in range(low_levels):
        chain = fan_out(chain, top_count * rank)
    for leaf in range(leaf_dev):
        for number in range(top_count):
            begin = (leaf * top_count + number) * rank
            both = split(chain[begin : begin + rank])
            for half in range(2):
                wpath[
                    (2 * number + half) * rank : (2 * number + half + 1) * rank,
                    2 * rank * leaf : 2 * rank * (leaf + 1),
                ] = both

    ones = [(relay_first, leaf) for leaf in range(leaf_dev)]
    twos = [(relay_second, leaf) for leaf in range(turned)]
    plan_outer, plan_soon, plan_inner = relay_plan(leaf_dev, turned, relayed)

    def relays(point):
        steps = [ones[leaf] if kind == 0 else twos[leaf] for kind, leaf in plan_outer[point]]
        soon = [leaf for _, leaf in plan_soon[point]]
        if steps:
            @pl.when(outer & jnp.logical_not(early))
            def _():
                for step, leaf in steps:
                    step(leaf)

        if soon:
            @pl.when(outer & early)
            def _():
                for leaf in soon:
                    relay_first(leaf)

        late = plan_inner[point]
        if late:
            @pl.when(jnp.logical_not(outer))
            def _():
                for leaf in late:
                    relay_first(leaf)

    if rounds > 0:
        with mark("06known"):
            get_known(1)
        if rounds > 1:
            make_known(2)
    with mark("07p0"):
        relays(0)

    locals_low = []
    level_vals, level_id = moment0, 0
    while (leaf_dev >> level_id) >= 4:
        if level_id:
            level_vals = lift(level_vals, 2)
        count = leaf_dev >> level_id
        locals_low.append(
            couple(
                [
                    [level_vals[c // 4 * 4 + (c + offset) % 4] for offset in range(1, 4)]
                    for c in range(count)
                ],
                [row_starts[level_id] + me * count + c for c in range(count)],
            )
        )
        level_id += 1
        if level_id == 1:
            pl.when(jnp.logical_not(outer))(functools.partial(send_across, range(leaf_dev)))
            with mark("08p1"):
                relays(1)
    with mark("09arecv"):
        pltpu.make_async_copy(
            buf_a.at[pl.ds(0, block // 2 - 1)], buf_a.at[pl.ds(0, block // 2 - 1)],
            a_recv.at[0],
        ).wait()
    for k in range(2, block, 2):
        remote(
            buf_a.at[mine ^ k], buf_a.at[mine ^ k], sent_sem.at[0], a_recv.at[1], me ^ 1
        ).start()
    with mark("08p2"):
        relays(2)
    pl.when(z_have & jnp.logical_not(outer))(
        functools.partial(send_beyond, range(relayed, 3))
    )
    with mark("09brecv"):
        pltpu.make_async_copy(
            buf_a.at[pl.ds(0, block // 2)], buf_a.at[pl.ds(0, block // 2)], a_recv.at[1]
        ).wait()
    eight = [buf_a[p] for p in range(block)]
    buf6[own_block] = lift(eight, block)[0]
    with mark("10known"):
        for r in range(2, rounds + 1):
            get_known(r)
            if r < rounds:
                make_known(r + 1)
    with mark("10bsend"):
        for k in range(block_count - 1, 1, -1):
            remote(
                buf6.at[own_block], buf6.at[own_block], sent_sem.at[0], far_recv.at[1],
                (own_block ^ k) * block + mine,
            ).start()
    with mark("11p3"):
        relays(3)
    five = lift(eight, block // 2)
    for p in range(2):
        buf5[p] = five[p]
    q_copy = remote(
        buf5.at[pl.ds(0, 2)], buf5.at[pl.ds(2, 2)], sent_sem.at[0], far_recv.at[2],
        (own_block + 1 - 2 * lax.rem(own_block, 2)) * block + mine,
    )
    q_copy.start()
    pl.when(z_have & jnp.logical_not(outer))(
        functools.partial(send_beyond, range(3, leaf_dev))
    )
    if kept < leaf_dev:
        pl.when(z_have & outer)(functools.partial(send_beyond, range(kept, leaf_dev)))
    with mark("11p4"):
        relays(4)
    for p, part in enumerate(lift(eight, 2)):
        buf4[p] = part

    with mark("12pair"):
        pair_copy.wait_recv()
    members2 = two + [pair2[1, 0], pair2[1, 1]]
    groups = [[members2[(c + offset) % 4] for offset in range(1, 4)] for c in range(2)]
    rows = [row_starts[level_id] + me * 2 + c for c in range(2)]
    level_id += 1
    groups.append(
        [buf_a[upper * sub + lax.rem(place_sub + offset, 4)] for offset in range(1, 4)]
    )
    rows.append(row_starts[level_id] + me)
    groups.append([buf4[lax.rem(mine // 2 + offset, 4)] for offset in range(1, 4)])
    rows.append(row_starts[level_id + 1] + me // 2)
    with mark("13p5"):
        relays(5)
    middle = couple(groups, rows)
    locals_low.append(middle[: 2 * rhs])
    field = middle[2 * rhs : 3 * rhs] + descend(middle[3 * rhs :], 0)
    with mark("13p6"):
        relays(6)
    for step in range(len(locals_low) - 1, -1, -1):
        field = locals_low[step] + fan_out(field, rhs)
        with mark("13p7"):
            relays(7 + len(locals_low) - 1 - step)

    with mark("15nearload"):
        pltpu.make_async_copy(nb, nb, load_sem.at[0]).wait()
    with mark("16first"):
        first = [nt(joined(leaf), nb[leaf, 0]) for leaf in range(leaf_dev)]
    with mark("17p10"):
        relays(10)
    with mark("19qwait"):
        q_copy.wait_recv()
    buf6[own_block ^ 1] = lift([buf5[2], buf5[3]], 2)[0]

    def add_far(base):
        with mark("18brecv"):
            pltpu.make_async_copy(
                buf6.at[pl.ds(0, block_count - 2)], buf6.at[pl.ds(0, block_count - 2)], far_recv.at[1]
            ).wait()
        groups = [[buf5[lax.rem(upper + offset, 4)] for offset in range(1, 4)]]
        rows = [row_starts[level_id + 2] + me // sub]
        first_six = level_id + 3
        start, span, level = 0, block_count, first_six
        while True:
            own = own_block >> (level - first_six)
            groups.append(
                [
                    buf6[start + own // 4 * 4 + lax.rem(lax.rem(own, 4) + offset, 4)]
                    for offset in range(1, 4)
                ]
            )
            rows.append(row_starts[level] + own)
            if span <= 4:
                break
            for p, part in enumerate(lift([buf6[start + p] for p in range(span)], 2)):
                buf6[start + span + p] = part
            start, span, level = start + span, span // 2, level + 1
        groups, rows = groups[::-1], rows[::-1]
        with mark("20top"):
            top = split(couple(groups, rows))
            top = jnp.concatenate([top[p * rhs : (p + 1) * rhs] for p in range(top_count)], axis=1)
            spread = nn(top, wpath[...])
        partial = []
        for leaf in range(leaf_dev):
            whole = split(
                field[leaf * rhs : (leaf + 1) * rhs]
                + fold(spread[:, 2 * rank * leaf : 2 * rank * (leaf + 1)], rank)
            )
            twice = jnp.concatenate([bas[leaf], bas[leaf]], axis=0)
            partial.append(base[leaf] + nn(whole, twice))
        return partial

    def add_near(base):
        total = base
        for half in range(2):
            begin = half * middle_leaf
            group = range(begin, begin + middle_leaf)
            with mark(f"21wait{half}"):
                @pl.when(jnp.logical_not(outer))
                def _(group=group):
                    for leaf in group:
                        if leaf >= relayed:
                            y_wait(leaf)

                @pl.when(z_have & jnp.logical_not(second_turn))
                def _(group=group):
                    for leaf in group:
                        if leaf < turned:
                            z_wait(leaf)

                if half:
                    @pl.when(z_have)
                    def _():
                        count = leaf_dev - turned
                        pltpu.make_async_copy(
                            src.at[:, pl.ds(0, points * count)], src.at[:, pl.ds(0, points * count)],
                            z_recv.at[turned],
                        ).wait()

            with mark(f"22near{half}"):
                for number, step in enumerate((-1, 1)):
                    @pl.when(me > 0 if step < 0 else me < devices - 1)
                    def _(number=number, step=step, half=half):
                        pltpu.make_async_copy(
                            bufs[half].at[2 + step], bufs[half].at[2 + step],
                            near_recv.at[number, half],
                        ).wait()
            with mark(f"23sum{half}"):
                added = []
                for leaf in range(leaf_dev):
                    acc = total[leaf]
                    for s in range(1, near):
                        index = near_pat[s, leaf]
                        gap = index // leaf_dev - me
                        place = jnp.where(
                            gap == -sub, 0,
                            jnp.where(
                                gap == -1, 1,
                                jnp.where(gap == 0, 2, jnp.where(gap == 1, 3, 4)),
                            ),
                        )
                        acc = acc + nt(
                            bufs[half][place, lax.rem(index, leaf_dev)],
                            nb[leaf, s, :, short * half : short * (half + 1)],
                        )
                    added.append(acc)
                total = added
        return total

    def store(total):
        for leaf in range(leaf_dev):
            out[:, points * leaf : points * (leaf + 1)] = total[leaf].astype(out.dtype)

    @pl.when(z_have)
    def _():
        store(add_near(add_far(first)))

    @pl.when(jnp.logical_not(z_have))
    def _():
        store(add_far(add_near(first)))

    inner = jnp.logical_not(outer)
    sent = (
        (0, me >= 0, leaf_dev), (1, place_sub < sub - 1, leaf_dev), (2, place_sub > 0, leaf_dev),
        (3, z_send & outer, kept), (3, z_send & inner, relayed),
        (4, first_turn, leaf_dev), (4, second_turn, turned),
        (5, z_have & inner, leaf_dev - relayed), (5, z_have & outer, leaf_dev - kept), (6, skip_turn, leaf_dev - turned),
    )
    for number, condition, count in sent:
        if count == 0:
            continue

        @pl.when(condition)
        def _(number=number, count=count):
            pltpu.make_async_copy(
                src.at[:, pl.ds(0, points * count)], src.at[:, pl.ds(0, points * count)],
                sent_sem.at[0],
            ).wait()
    pltpu.make_async_copy(
        buf_a.at[pl.ds(0, block - 1)], buf_a.at[pl.ds(0, block - 1)], sent_sem.at[0]
    ).wait()
    pltpu.make_async_copy(
        buf6.at[pl.ds(0, block_count - 2)], buf6.at[pl.ds(0, block_count - 2)], sent_sem.at[0]
    ).wait()
    pair_copy.wait_send()
    q_copy.wait_send()


def shards(sizes, sources, leaf_basis, transfer, coupling, near_blocks, near_pattern, far_pattern):
    sub, devices = sizes
    leaf_dev, points, rank = leaf_basis.shape
    rhs = sources.shape[1]
    near = near_blocks.shape[1]
    block = 2 * sub
    block_count = devices // block
    top_count = block_count.bit_length() - 1
    vmem = pl.BlockSpec(memory_space=pltpu.VMEM)
    hbm = pl.BlockSpec(memory_space=pl.ANY)
    dma = pltpu.SemaphoreType.DMA
    result = pl.pallas_call(
        functools.partial(kernel, (sub, devices, leaf_dev, near)),
        out_shape=pltpu.VMEM((rhs, leaf_dev * points), BF),
        in_specs=[hbm] * 7,
        out_specs=vmem,
        scratch_shapes=[
            pltpu.VMEM((5, leaf_dev, rhs, points // 2), BF),
            pltpu.VMEM((5, leaf_dev, rhs, points // 2), BF),
            pltpu.VMEM((leaf_dev, rank, points), BF),
            pltpu.VMEM((leaf_dev, near, points, points), BF),
            pltpu.VMEM((leaf_dev, rhs, 2 * rank), BF),
            pltpu.VMEM((block, rhs, 2 * rank), BF),
            pltpu.VMEM((2, 2, rhs, 2 * rank), BF),
            pltpu.VMEM((4, rhs, 2 * rank), BF),
            pltpu.VMEM((4, rhs, 2 * rank), BF),
            pltpu.VMEM((2 * block_count, rhs, 2 * rank), BF),
            pltpu.VMEM((2, 2 * rank, 2 * rank), BF),
            pltpu.VMEM((2 * top_count * rank, 2 * rank * leaf_dev), BF),
            pltpu.VMEM(transfer.shape, F32),
            pltpu.VMEM(coupling.shape, F32),
            pltpu.SMEM(near_pattern.shape[::-1], jnp.int32),
            pltpu.SMEM(far_pattern.shape[::-1], jnp.int32),
            dma((4,)),
            dma((1,)),
            dma((2, 2)),
            dma((leaf_dev,)),
            dma((leaf_dev // 2 + 2,)),
            dma((2,)),
            dma((3,)),
            pltpu.SemaphoreType.REGULAR((max(block_count - 2, 1), 2)),
            pltpu.SemaphoreType.REGULAR((1,)),
        ],
        compiler_params=pltpu.CompilerParams(collective_id=0, has_side_effects=True),
    )(
        sources.T,
        leaf_basis.transpose(0, 2, 1),
        transfer,
        coupling,
        near_blocks,
        near_pattern.T,
        far_pattern.T,
    )
    return result.T


def solution(mesh):
    placed = (
        P(("leaf", "sub"), None),
        P(("leaf", "sub"), None, None),
        P(),
        P(),
        P(("leaf", "sub"), None, None, None),
        P(("leaf", "sub"), None),
        P(),
    )
    sizes = (mesh.shape["sub"], mesh.shape["leaf"] * mesh.shape["sub"])
    return jax.shard_map(
        functools.partial(shards, sizes),
        mesh=mesh, in_specs=placed, out_specs=P(("leaf", "sub"), None), check_vma=False,
    )
```
